32 devices in a mesh: mode: 8 (over z, y), tm: 4 (over x, core).
Axes of the slice: x: 2, y: 2, z: 4, core: 2. Of those that a mesh axis runs over, the one named last changes fastest.
Arguments:
- support_accel: bfloat16 [512, 2048], P(None, 'tm'), may hold values from -6 to 6
- participation: bfloat16 [2048, 512], P('mode'), may hold values from -0.25 to 0.25
- kernels: float32 [2048, 2048], P('mode'), may hold values from -0.25 to 0.25
- lengths: int32 [2048], P('mode'), may hold values from 1 to 2048, as said below
- mode_shapes: bfloat16 [16384, 2048], P('mode'), may hold values from -0.125 to 0.125
- groups: int32 [16384], P('mode'), may hold values from 0 to 511
Outputs:
- response: bfloat16 [16384, 2048], P('mode', 'tm')
The draws below stay inside these ranges and needn't reach their ends.
Inputs may be any that keep to these rules, and one draw needn't show every extreme that they name: `lengths`: some mode has exactly 2048 taps in every draw.
All inputs are finite; a program needn't handle non-finite values.
Results may differ from the reference program's by a relative error of at most 0.0033.
Values may be sent and summed in bfloat16 or wider, within the bound.
A program may use at most 64 MiB of HBM per device.

```python
import math
import jax
import jax.numpy as jnp
from jax import lax

MODES = 2048
SUPPORTS = 512
LMAX = 2048
TIME = 2048
DOFS = 16384


def draw_lengths(key, part):
    first_key = jax.random.fold_in(key, 0)
    index = jnp.arange(MODES, dtype=jnp.int32)
    remain = MODES - index
    ceiling = remain * LMAX // MODES * remain // MODES
    ceiling = jnp.maximum(ceiling, 1)
    chosen = jax.random.randint(first_key, (MODES,), 1, ceiling + 1)
    chosen = jnp.where(index == 0, LMAX, chosen)
    return chosen.astype(jnp.int32)


def place_ends(result, rng, low, high):
    spot = [jax.random.randint(jax.random.fold_in(rng, axis), (), 0, length) for axis, length in enumerate(result.shape)]
    main_axis = result.shape.index(max(result.shape))
    next_to = spot[:main_axis] + [(spot[main_axis] + 1) % result.shape[main_axis]] + spot[main_axis + 1:]
    return result.at[tuple(spot)].set(low).at[tuple(next_to)].set(high)


def level_of(rng, dims, cuts, smallest, top_value):
    level = 1.0
    for axis_at, shards_of in cuts:
        steps = jax.random.uniform(jax.random.fold_in(jax.random.fold_in(rng, 6), axis_at), (shards_of,), jnp.float32, smallest / len(cuts), top_value / len(cuts))
        level = level * jnp.repeat(jnp.exp(steps), dims[axis_at] // shards_of).reshape((-1,) + (1,) * (len(dims) - 1 - axis_at))
    return level


def centred(key, dims, deviation, reach, cuts=(), held_as=jnp.bfloat16):
    entries = deviation * jax.random.normal(key, dims, jnp.float32)
    if cuts:
        entries = entries * level_of(key, dims, cuts, -0.22, 0.18)
    return jnp.clip(entries, -reach, reach).astype(held_as)


def setup_inputs(seed: int = 0) -> dict:
    arg_keys = jax.random.split(jax.random.key(seed), 7)
    return {
        "support_accel": centred(arg_keys[0], (SUPPORTS, TIME), 1.0, 6.0, ((1, 4),)),
        "participation": centred(arg_keys[1], (MODES, SUPPORTS), SUPPORTS ** -0.5, 0.25, ((0, 8),)),
        "kernels": centred(arg_keys[2], (MODES, LMAX), (LMAX // 4) ** -0.5, 0.25, ((0, 8),), jnp.float32),
        "lengths": draw_lengths(jax.random.fold_in(arg_keys[6], 71), 0),
        "mode_shapes": centred(arg_keys[4], (DOFS, MODES), MODES ** -0.5, 0.125, ((0, 8),)),
        "groups": place_ends(jax.random.randint(arg_keys[5], (DOFS,), 0, SUPPORTS), jax.random.fold_in(arg_keys[5], 1), 0, SUPPORTS - 1).astype(jnp.int32),
    }


def reference(support_accel, participation, kernels, lengths, mode_shapes, groups):
    forces = jnp.dot(participation, support_accel, preferred_element_type=jnp.float32)
    alive = jnp.arange(LMAX, dtype=jnp.int32)[None, :] < lengths[:, None]
    masked = jnp.where(alive, kernels, jnp.zeros_like(kernels))
    length_fft = TIME + LMAX
    spectrum = jnp.fft.rfft(forces, n=length_fft, axis=1) * jnp.fft.rfft(masked, n=length_fft, axis=1)
    modal = jnp.fft.irfft(spectrum, n=length_fft, axis=1)[:, :TIME].astype(jnp.bfloat16)
    rows_block = math.gcd(DOFS, 4096)
    shaped = mode_shapes.reshape(DOFS // rows_block, rows_block, MODES)
    grouped = groups.reshape(DOFS // rows_block, rows_block)

    def expand(pair):
        shapes_block, groups_block = pair
        summed = jnp.dot(shapes_block, modal, preferred_element_type=jnp.float32)
        ground = jnp.take(support_accel, groups_block, axis=0).astype(jnp.float32)
        return (summed + ground).astype(jnp.bfloat16)

    return lax.map(expand, (shaped, grouped)).reshape(DOFS, TIME)
```

```python
import collections
import functools

import jax
import jax.numpy as jnp
import numpy as np
from jax import lax
from jax.experimental import pallas as pl
from jax.experimental.pallas import tpu as pltpu
from jax.sharding import PartitionSpec as P

BLOCK = 128
F32 = jnp.float32
BF16 = jnp.bfloat16
MESH = pl.DeviceIdType.MESH


def split_constant(table):
    high = table.astype(BF16)
    low = (table - high.astype(np.float64)).astype(BF16)
    return high, low


def transform_tables():
    angle = np.pi * (np.arange(BLOCK)[:, None] + 0.5) / BLOCK
    time = np.arange(2 * BLOCK)[None, :]
    cos, sin = np.cos(angle * time), np.sin(angle * time)
    forward = np.concatenate([cos[:, :BLOCK], -sin[:, :BLOCK]], axis=0).T
    backward = np.concatenate([cos, -sin], axis=0) / BLOCK
    return split_constant(forward) + split_constant(backward)


def dot3(values, high, low):
    top = values.astype(BF16)
    rest = (values - top.astype(F32)).astype(BF16)
    dot = functools.partial(jnp.dot, preferred_element_type=F32)
    return dot(top, high) + (dot(rest, high) + dot(top, low))


def grid_of(groups, ways):
    ny = max(ways // 2, 1)
    if groups % ny:
        ny = 1
    return ny, groups // ny


def last_group(i, ny, nz):
    z, y = i // ny, lax.rem(i, ny)
    far = jnp.where(2 * z < nz, nz - 1, 0)
    return far * ny + lax.rem(y + 1, ny)


def taps_spectrum(first, k_own, len_ref, xs, hs, fh_ref, fl_ref):
    rows, taps = k_own.shape
    held = len_ref.shape[1]
    picked = lax.broadcasted_iota(jnp.int32, (rows, held), 1) == first + lax.broadcasted_iota(jnp.int32, (rows, held), 0)
    wide = jnp.broadcast_to(len_ref[...], (rows, held)).astype(F32)
    lengths = jnp.sum(jnp.where(picked, wide, 0.0), axis=1, keepdims=True)
    kblocks = taps // BLOCK
    for c in range(kblocks):
        pos = (c * BLOCK + lax.broadcasted_iota(jnp.int32, (rows, BLOCK), 1)).astype(F32)
        part = k_own[:, c * BLOCK:(c + 1) * BLOCK]
        xs[c * rows:(c + 1) * rows, :] = jnp.where(pos < lengths, part, jnp.zeros_like(part))
    hs[...] = dot3(xs[:kblocks * rows, :], fh_ref[...], fl_ref[...])


def filter_rows(f_ref, m_ref, kblocks, xs, fs, hs, fh_ref, fl_ref, bh_ref, bl_ref):
    ways, rows, slab = f_ref.shape
    per = slab // BLOCK
    tblocks = ways * per
    for a in range(tblocks):
        at = (a % per) * BLOCK
        xs[a * rows:(a + 1) * rows, :] = f_ref[a // per, :, at:at + BLOCK]
    fs[...] = dot3(xs[:tblocks * rows, :], fh_ref[...], fl_ref[...])
    before = jnp.zeros((rows, BLOCK), F32)
    for b in range(tblocks):
        re = jnp.zeros((rows, BLOCK), F32)
        im = jnp.zeros((rows, BLOCK), F32)
        for c in range(min(b + 1, kblocks)):
            fr = fs[(b - c) * rows:(b - c + 1) * rows, :BLOCK]
            fi = fs[(b - c) * rows:(b - c + 1) * rows, BLOCK:]
            hr = hs[c * rows:(c + 1) * rows, :BLOCK]
            hi = hs[c * rows:(c + 1) * rows, BLOCK:]
            re = re + (fr * hr - fi * hi)
            im = im + (fr * hi + fi * hr)
        wide = dot3(jnp.concatenate([re, im], axis=1), bh_ref[...], bl_ref[...])
        at = (b % per) * BLOCK
        m_ref[b // per, :, at:at + BLOCK] = (before + wide[:, :BLOCK]).astype(BF16)
        before = wide[:, BLOCK:]


def when(cond, body):
    if cond is None:
        body()
    else:
        pl.when(cond)(body)


def both(a, b):
    if a is None:
        return b
    return a if b is None else a & b


def main_kernel(
    ny, tile, a_hbm, p_hbm, k_hbm, len_hbm, s_hbm, g_hbm, fh_hbm, fl_hbm, bh_hbm, bl_hbm,
    acc_ref, big, slast_ref,
    a_ref, p_ref, len_ref, g_ref, fh_ref, fl_ref, bh_ref, bl_ref, in_sem,
    k_own, shapes, fsend, frecv, mod, xs, fs, hs, hot,
    k_sem, shape_sem, slast_sem, f_send, f_recv, own_sem, m_send, recv, s_up, s_down, s_y, s_relief,
):
    groups, ways, share, slab = big.shape
    dofs = acc_ref.shape[0]
    per_group = ways * share
    nz = groups // ny
    split = shapes.shape[0] == groups
    i, j = lax.axis_index("mode"), lax.axis_index("tm")
    z, y = i // ny, lax.rem(i, ny)
    below, above = z > 0, z < nz - 1
    relief = ny == 2 and nz % 2 == 0 and ways >= 4

    def peer(d):
        return lax.rem(j // 2 + d // 2, ways // 2) * 2 + (lax.rem(j, 2) + d) % 2 if ways > 1 else j

    loads = [
        pltpu.make_async_copy(src, dst, in_sem.at[n])
        for n, (src, dst) in enumerate((
            (a_hbm, a_ref), (p_hbm, p_ref), (len_hbm, len_ref), (fh_hbm, fh_ref), (fl_hbm, fl_ref),
            (g_hbm, g_ref), (bh_hbm, bh_ref), (bl_hbm, bl_ref),
        ))
    ]
    for load in loads:
        load.start()
    first = j * share
    k_copy = pltpu.make_async_copy(k_hbm.at[pl.ds(pl.multiple_of(first, share), share)], k_own, k_sem)
    k_copy.start()

    def columns(g):
        return s_hbm.at[:, pl.ds(pl.multiple_of(g * per_group, per_group), per_group)]

    glast = last_group(i, ny, nz)
    shape_copies = []
    if split:
        for d in range(groups):
            g = lax.rem(i + d, groups)
            shape_copies.append(pltpu.make_async_copy(columns(g), shapes.at[g], shape_sem.at[d]))
        shape_copies.append(pltpu.make_async_copy(columns(glast), slast_ref, slast_sem))
    else:
        shape_copies.append(pltpu.make_async_copy(s_hbm, shapes.at[0], shape_sem.at[0]))
    for copy in shape_copies:
        copy.start()

    barrier = pltpu.get_barrier_semaphore()

    def greet(mode, tm):
        pl.semaphore_signal(barrier, inc=1, device_id={"mode": mode, "tm": tm}, device_id_type=MESH)

    for d in range(1, ways):
        greet(i, lax.rem(j + d, ways))
    for e in range(1, ny):
        greet(z * ny + lax.rem(y + e, ny), j)

    if nz > 1:
        @pl.when(below)
        def _():
            greet(i - ny, j)

        @pl.when(above)
        def _():
            greet(i + ny, j)

    loads[0].wait()
    loads[1].wait()

    for d in range(ways):
        q = peer(ways - 1 - d)
        rows = p_ref[pl.ds(pl.multiple_of(q * share, share), share), :]
        fsend[q] = jnp.dot(rows, a_ref[...], preferred_element_type=F32)

    always = ways - 1 + ny - 1
    if nz == 1:
        pl.semaphore_wait(barrier, always)
    else:
        @pl.when(below & above)
        def _():
            pl.semaphore_wait(barrier, always + 2)

        @pl.when(jnp.logical_not(below & above))
        def _():
            pl.semaphore_wait(barrier, always + 1)

    force_copies = []
    for d in range(ways - 1, 0, -1):
        q = peer(d)
        force_copies.append((pltpu.make_async_remote_copy(
            fsend.at[q], frecv.at[j], f_send.at[d], f_recv.at[j],
            device_id={"mode": i, "tm": q}, device_id_type=MESH,
        ), q))
    for copy, _ in force_copies:
        copy.start()
    frecv[j] = fsend[j]

    for load in loads[2:]:
        load.wait()
    k_copy.wait()
    taps_spectrum(first, k_own, len_ref, xs, hs, fh_ref, fl_ref)
    kblocks = k_own.shape[1] // BLOCK

    lanes = g_ref.shape[1]
    eye = lax.broadcasted_iota(jnp.int32, (lanes, lanes), 0) == lax.broadcasted_iota(jnp.int32, (lanes, lanes), 1)

    def ground(r, carry):
        for part in range(tile // lanes):
            row = g_ref[pl.ds(r * (tile // lanes) + part, 1), :].astype(F32)
            column = jnp.sum(jnp.where(eye, jnp.broadcast_to(row, (lanes, lanes)), 0.0), axis=1, keepdims=True)
            support = lax.broadcasted_iota(jnp.int32, (lanes, a_ref.shape[0]), 1).astype(F32)
            hot[part * lanes:(part + 1) * lanes, :] = (support == column).astype(F32).astype(BF16)
        at = pl.ds(pl.multiple_of(r * tile, tile), tile)
        acc_ref[at, :] = jnp.dot(hot[...], a_ref[...], preferred_element_type=F32)
        return carry

    lax.fori_loop(0, dofs // tile, ground, 0)

    for d in range(1, ways):
        q = peer(d)
        pltpu.make_async_remote_copy(
            fsend.at[q], frecv.at[q], f_send.at[d], f_recv.at[q],
            device_id={"mode": i, "tm": q}, device_id_type=MESH,
        ).wait_recv()
    filter_rows(frecv, mod, kblocks, xs, fs, hs, fh_ref, fl_ref, bh_ref, bl_ref)

    pending = []

    def send(cond, src, g, q, sem, mode, tm):
        def make():
            return pltpu.make_async_remote_copy(
                src, big.at[g, q], sem, recv.at[g, q], device_id={"mode": mode, "tm": tm}, device_id_type=MESH,
            )
        when(cond, lambda: make().start())
        pending.append((cond, make))

    def arrived(cond, g, q):
        when(cond, lambda: pltpu.make_async_remote_copy(
            big.at[g, q], big.at[g, q], own_sem, recv.at[g, q],
            device_id={"mode": i, "tm": j}, device_id_type=MESH,
        ).wait_recv())

    work = collections.deque()

    def product(cond, g):
        if not split:
            return

        def unit(r):
            at = pl.ds(r * tile, tile)
            block = big[g].reshape(per_group, slab)
            acc_ref[at, :] += jnp.dot(shapes[g, at, :], block, preferred_element_type=F32)
        for r in range(dofs // tile):
            work.append((cond, functools.partial(unit, r)))

    def drain(n):
        for _ in range(min(n, len(work))):
            cond, unit = work.popleft()
            when(cond, unit)

    def across(cond, src, g, q, slot, d):
        for e in range(1, ny):
            send(cond, src, g, q, s_y.at[slot, e - 1, d], z * ny + lax.rem(y + e, ny), j)

    def up(src, g, q, slot, d, cond=None):
        if nz > 1:
            send(both(cond, above), src, g, q, s_up.at[slot, d], i + ny, j)

    def down(src, g, q, slot, d, cond=None):
        if nz > 1:
            send(both(cond, below), src, g, q, s_down.at[slot, d], i - ny, j)

    own = pltpu.make_async_copy(mod.at[j], big.at[i, j], own_sem)
    across(None, mod.at[j], i, j, 0, 0)
    up(mod.at[j], i, j, 0, 0)
    down(mod.at[j], i, j, 0, 0)
    for d in range(ways - 1, 0, -1):
        q = peer(d)
        pending.append((None, functools.partial(
            pltpu.make_async_remote_copy, mod.at[q], big.at[i, j], m_send.at[d], recv.at[i, j],
            device_id={"mode": i, "tm": q}, device_id_type=MESH,
        )))
        pending[-1][1]().start()
    own.start()
    for copy in shape_copies:
        copy.wait()
    own.wait()
    for d in range(1, ways):
        q = peer(d)
        arrived(None, i, q)
        across(None, big.at[i, q], i, q, 0, d)
        up(big.at[i, q], i, q, 0, d)
        down(big.at[i, q], i, q, 0, d)
    product(None, i)

    partner = z + 1 - 2 * lax.rem(z, 2)
    for s in range(1, nz + 1):
        lower, upper = i - s * ny, i + s * ny
        has_low, has_high = z - s >= 0, z + s <= nz - 1
        for d in range(ways):
            q = peer(d)
            if s < nz:
                crossing = None
                if relief and s == 1 and d < 2:
                    crossing = z - 1 != partner
                arrived(has_low, lower, q)
                up(big.at[lower, q], lower, q, s, d, has_low)
                across(both(has_low, crossing), big.at[lower, q], lower, q, s, d)
                if relief and s == 1 and d < 2:
                    crossing = z + 1 != partner
                arrived(has_high, upper, q)
                down(big.at[upper, q], upper, q, s, d, has_high)
                across(both(has_high, crossing), big.at[upper, q], upper, q, nz - 1 + s, d)
            for e in range(1, ny):
                line = lax.rem(y + e, ny)
                if s == 1:
                    g = z * ny + line
                    arrived(None, g, q)
                    if relief and d < 2:
                        send(None, big.at[g, q], g, q, s_relief.at[d], partner * ny + y, j)
                else:
                    arrived(z - s + 1 >= 0, (z - s + 1) * ny + line, q)
                    arrived(z + s - 1 <= nz - 1, (z + s - 1) * ny + line, q)
            drain(3)
        if s < nz:
            product(has_low, lower)
            product(has_high, upper)
        for e in range(1, ny):
            line = lax.rem(y + e, ny)
            if s == 1:
                g = z * ny + line
                product(g != glast, g)
            else:
                g = (z - s + 1) * ny + line
                product((z - s + 1 >= 0) & (g != glast), g)
                g = (z + s - 1) * ny + line
                product((z + s - 1 <= nz - 1) & (g != glast), g)
    drain(len(work))
    if not split:
        def whole(r, carry):
            at = pl.ds(pl.multiple_of(r * tile, tile), tile)
            block = big[...].reshape(groups * per_group, slab)
            acc_ref[at, :] += jnp.dot(shapes[0, at, :], block, preferred_element_type=F32)
            return carry
        lax.fori_loop(0, dofs // tile, whole, 0)
    for copy, _ in force_copies:
        copy.wait_send()
    for cond, make in pending:
        when(cond, lambda: make().wait_send())


def tail_kernel(ny, acc_ref, big, s_ref, o_ref):
    groups, ways, share, slab = big.shape
    glast = last_group(lax.axis_index("mode"), ny, groups // ny)
    tile = o_ref.shape[0]
    at = pl.ds(pl.multiple_of(pl.program_id(0) * tile, tile), tile)
    total = acc_ref[at, :]
    if s_ref.shape[0] > tile:
        block = big[glast].reshape(ways * share, slab)
        total += jnp.dot(s_ref[at, :], block, preferred_element_type=F32)
    o_ref[...] = total.astype(BF16)


def per_device(support_accel, participation, kernels, lengths, mode_shapes, groups):
    ways, ngroups = lax.axis_size("tm"), lax.axis_size("mode")
    ny, nz = grid_of(ngroups, ways)
    held, taps = kernels.shape
    share = held // ways
    supports, slab = support_accel.shape
    dofs, modes = mode_shapes.shape
    tile = min(512, dofs)
    split = held % 128 == 0 and ny > 1 and dofs > tile
    times = ways * slab
    tables = transform_tables()
    vmem = pl.BlockSpec(memory_space=pltpu.VMEM)
    hbm = pl.BlockSpec(memory_space=pltpu.HBM)
    dma = pltpu.SemaphoreType.DMA
    acc, every, shapes = pl.pallas_call(
        functools.partial(main_kernel, ny, tile),
        out_shape=(
            pltpu.VMEM((dofs, slab), F32),
            pltpu.VMEM((ngroups, ways, share, slab), BF16),
            pltpu.VMEM((dofs, held) if split else (16, 128), BF16),
        ),
        in_specs=[hbm] * 10,
        out_specs=(vmem, vmem, vmem),
        scratch_shapes=[
            pltpu.VMEM((supports, slab), BF16),
            pltpu.VMEM((held, supports), BF16),
            pltpu.VMEM((1, held), jnp.int32),
            pltpu.VMEM((dofs // 128, 128), jnp.int32),
            *(pltpu.VMEM(table.shape, BF16) for table in tables),
            dma((8,)),
            pltpu.VMEM((share, taps), F32),
            pltpu.VMEM((ngroups, dofs, held) if split else (1, dofs, modes), BF16),
            pltpu.VMEM((ways, share, slab), F32),
            pltpu.VMEM((ways, share, slab), F32),
            pltpu.VMEM((ways, share, slab), BF16),
            pltpu.VMEM((max(times, taps) // BLOCK * share, BLOCK), F32),
            pltpu.VMEM((times // BLOCK * share, 2 * BLOCK), F32),
            pltpu.VMEM((taps // BLOCK * share, 2 * BLOCK), F32),
            pltpu.VMEM((tile, supports), BF16),
            dma, dma((ngroups,)), dma, dma((ways,)), dma((ways,)), dma, dma((ways,)), dma((ngroups, ways)),
            dma((nz, ways)), dma((nz, ways)), dma((2 * nz - 1, max(ny - 1, 1), ways)), dma((2,)),
        ],
        compiler_params=pltpu.CompilerParams(
            collective_id=0, has_side_effects=True, vmem_limit_bytes=32 << 20
        ),
    )(*(pltpu.with_memory_space_constraint(array, pltpu.HBM) for array in (
        support_accel, participation, kernels, lengths.reshape(1, held), mode_shapes,
        groups.reshape(dofs // 128, 128), *map(jnp.asarray, tables),
    )))
    return pl.pallas_call(
        functools.partial(tail_kernel, ny),
        grid=(dofs // tile,),
        out_shape=jax.ShapeDtypeStruct((dofs, slab), BF16),
        in_specs=[vmem, vmem, vmem],
        out_specs=pl.BlockSpec((tile, slab), lambda r: (r, 0)),
        compiler_params=pltpu.CompilerParams(vmem_limit_bytes=32 << 20),
    )(acc, every, shapes)


def solution(mesh):
    placed = (
        P(None, "tm"),
        P("mode", None),
        P("mode", None),
        P("mode"),
        P("mode", None),
        P("mode"),
    )
    return jax.shard_map(
        per_device, mesh=mesh, in_specs=placed, out_specs=P("mode", "tm"), check_vma=False
    )
```

```python
import collections
import functools

import jax
import jax.numpy as jnp
import numpy as np
from jax import lax
from jax.experimental import pallas as pl
from jax.experimental.pallas import tpu as pltpu
from jax.sharding import PartitionSpec as P

BLOCK = 128
F32 = jnp.float32
BF16 = jnp.bfloat16
MESH = pl.DeviceIdType.MESH


def split_constant(table):
    high = table.astype(BF16)
    low = (table - high.astype(np.float64)).astype(BF16)
    return high, low


def transform_tables():
    angle = np.pi * (np.arange(BLOCK)[:, None] + 0.5) / BLOCK
    time = np.arange(2 * BLOCK)[None, :]
    cos, sin = np.cos(angle * time), np.sin(angle * time)
    forward = np.concatenate([cos[:, :BLOCK], -sin[:, :BLOCK]], axis=0).T
    backward = np.concatenate([cos, -sin], axis=0) / BLOCK
    return split_constant(forward) + split_constant(backward)


def dot3(values, high, low):
    top = values.astype(BF16)
    rest = (values - top.astype(F32)).astype(BF16)
    dot = functools.partial(jnp.dot, preferred_element_type=F32)
    return dot(top, high) + (dot(rest, high) + dot(top, low))


def grid_of(groups, ways):
    ny = max(ways // 2, 1)
    if groups % ny:
        ny = 1
    return ny, groups // ny


def last_group(i, ny, nz):
    z, y = i // ny, lax.rem(i, ny)
    far = jnp.where(2 * z < nz, nz - 1, 0)
    return far * ny + lax.rem(y + 1, ny)


def column_of(row, rows):
    lanes = row.shape[1]
    at = lax.broadcasted_iota(jnp.int32, (rows, lanes), 0) == lax.broadcasted_iota(jnp.int32, (rows, lanes), 1)
    return jnp.sum(jnp.where(at, jnp.broadcast_to(row, (rows, lanes)), 0.0), axis=1, keepdims=True)


def row_of(column, lanes):
    rows = column.shape[0]
    at = lax.broadcasted_iota(jnp.int32, (rows, lanes), 0) == lax.broadcasted_iota(jnp.int32, (rows, lanes), 1)
    return jnp.sum(jnp.where(at, jnp.broadcast_to(column, (rows, lanes)), 0.0), axis=0, keepdims=True)


def taps_spectrum(first, k_own, len_ref, xs, hs, fh_ref, fl_ref):
    share, taps = k_own.shape
    chunks = hs.shape[0]
    rows = share // chunks
    held = len_ref.shape[1]
    picked = lax.broadcasted_iota(jnp.int32, (share, held), 1) == first + lax.broadcasted_iota(jnp.int32, (share, held), 0)
    wide = jnp.broadcast_to(len_ref[...], (share, held)).astype(F32)
    lengths = jnp.sum(jnp.where(picked, wide, 0.0), axis=1, keepdims=True)
    kblocks = taps // BLOCK
    for c in range(kblocks):
        pos = (c * BLOCK + lax.broadcasted_iota(jnp.int32, (share, BLOCK), 1)).astype(F32)
        part = k_own[:, c * BLOCK:(c + 1) * BLOCK]
        part = jnp.where(pos < lengths, part, jnp.zeros_like(part))
        for h in range(chunks):
            xs[h, c * rows:(c + 1) * rows, :] = part[h * rows:(h + 1) * rows, :]
    for h in range(chunks):
        hs[h] = dot3(xs[h, :kblocks * rows, :], fh_ref[...], fl_ref[...])


def filter_rows(blocks, store, hs, xs, fs, ws, fh_ref, fl_ref, bh_ref, bl_ref):
    tblocks = len(blocks)
    rows = blocks[0].shape[0]
    kblocks = hs.shape[0] // rows
    for a in range(tblocks):
        xs[a * rows:(a + 1) * rows, :] = blocks[a]
    fs[...] = dot3(xs[:tblocks * rows, :], fh_ref[...], fl_ref[...])
    for b in range(tblocks):
        re = jnp.zeros((rows, BLOCK), F32)
        im = jnp.zeros((rows, BLOCK), F32)
        for c in range(min(b + 1, kblocks)):
            fr = fs[(b - c) * rows:(b - c + 1) * rows, :BLOCK]
            fi = fs[(b - c) * rows:(b - c + 1) * rows, BLOCK:]
            hr = hs[c * rows:(c + 1) * rows, :BLOCK]
            hi = hs[c * rows:(c + 1) * rows, BLOCK:]
            re = re + (fr * hr - fi * hi)
            im = im + (fr * hi + fi * hr)
        ws[b * rows:(b + 1) * rows, :BLOCK] = re
        ws[b * rows:(b + 1) * rows, BLOCK:] = im
    wide = dot3(ws[...], bh_ref[...], bl_ref[...])
    for b in range(tblocks):
        y = wide[b * rows:(b + 1) * rows, :BLOCK]
        if b:
            y = y + wide[(b - 1) * rows:b * rows, BLOCK:]
        store(b, y.astype(BF16))


def when(cond, body):
    if cond is None:
        body()
    else:
        pl.when(cond)(body)


def both(a, b):
    if a is None:
        return b
    return a if b is None else a & b


LEVELS = 32000.0


def main_kernel(
    ny, tile, a_hbm, p_hbm, k_hbm, len_hbm, s_hbm, g_hbm, fh_hbm, fl_hbm, bh_hbm, bl_hbm,
    acc_ref, big, slast_ref,
    a_ref, p_ref, len_ref, g_ref, fh_ref, fl_ref, bh_ref, bl_ref, in_sem,
    k_own, shapes, forces, fcore, coded, codes, scaled, scales, steps, fall, mod, xs, xf, fs, hs, ws, hot,
    k_sem, shape_sem, slast_sem, core_send, core_recv, code_send, code_recv, scale_send, scale_recv, own_sem,
    m_send, recv, s_up0, s_down0, s_y0, s_up, s_down, s_y, s_relief,
):
    groups, ways, chunks, rows, slab = big.shape
    share = chunks * rows
    dofs = acc_ref.shape[0]
    per_group = ways * share
    nz = groups // ny
    split = shapes.shape[0] == groups
    i, j = lax.axis_index("mode"), lax.axis_index("tm")
    z, y = i // ny, lax.rem(i, ny)
    below, above = z > 0, z < nz - 1
    relief = ny == 2 and nz % 2 == 0 and ways >= 4
    mate = j + 1 - 2 * lax.rem(j, 2)

    def peer(d):
        return lax.rem(j // 2 + d // 2, ways // 2) * 2 + lax.rem(lax.rem(j, 2) + d, 2)

    loads = [
        pltpu.make_async_copy(src, dst, in_sem.at[n])
        for n, (src, dst) in enumerate((
            (a_hbm, a_ref), (p_hbm, p_ref), (len_hbm, len_ref), (fh_hbm, fh_ref), (fl_hbm, fl_ref),
            (bh_hbm, bh_ref), (bl_hbm, bl_ref), (g_hbm, g_ref),
        ))
    ]
    first = j * share
    k_copy = pltpu.make_async_copy(k_hbm.at[pl.ds(pl.multiple_of(first, share), share)], k_own, k_sem)
    for load in loads:
        load.start()
    k_copy.start()

    barrier = pltpu.get_barrier_semaphore()

    def greet(mode, tm):
        pl.semaphore_signal(barrier, inc=1, device_id={"mode": mode, "tm": tm}, device_id_type=MESH)

    for d in range(1, ways):
        greet(i, lax.rem(j + d, ways))
    for tm in (j, mate):
        for e in range(1, ny):
            greet(z * ny + lax.rem(y + e, ny), tm)
        if nz > 1:
            @pl.when(below)
            def _():
                greet(i - ny, tm)

            @pl.when(above)
            def _():
                greet(i + ny, tm)

    loads[0].wait()
    loads[1].wait()
    forces[...] = jnp.dot(p_ref[...], a_ref[...], preferred_element_type=F32)

    def forces_of(q):
        return forces[pl.ds(pl.multiple_of(q * share, share), share), :]

    lanes = scaled.shape[2]
    for d in range(2, ways):
        values = forces_of(peer(d))
        top = jnp.max(jnp.abs(values), axis=1, keepdims=True)
        scale = (top * 1.01 + 1e-30).astype(BF16)
        scaled[d] = jnp.broadcast_to(row_of(scale.astype(F32), lanes), scaled.shape[1:]).astype(BF16)
        values = values * (LEVELS / scale.astype(F32))
        values = jnp.round(values).astype(jnp.int32).astype(jnp.int16)
        for h in range(chunks):
            coded[d, h] = values[h * rows:(h + 1) * rows, :]

    always = ways - 1 + 2 * (ny - 1)
    if nz == 1:
        pl.semaphore_wait(barrier, always)
    else:
        @pl.when(below & above)
        def _():
            pl.semaphore_wait(barrier, always + 4)

        @pl.when(jnp.logical_not(below & above))
        def _():
            pl.semaphore_wait(barrier, always + 2)

    started = []

    def remote(src, dst, send_sem, recv_sem, mode, tm):
        return pltpu.make_async_remote_copy(
            src, dst, send_sem, recv_sem, device_id={"mode": mode, "tm": tm}, device_id_type=MESH,
        )

    def code_copy(d, h):
        return remote(coded.at[d, h], codes.at[d, h], code_send.at[d, h], code_recv.at[d, h], i, peer(d))

    def scale_copy(d):
        return remote(scaled.at[d], scales.at[d], scale_send.at[d], scale_recv.at[d], i, peer(d))

    core_copy = remote(forces.at[pl.ds(pl.multiple_of(mate * share, share), share)], fcore, core_send, core_recv, i, mate)
    for d in range(2, ways):
        scale_copy(d).start()
        started.append(functools.partial(scale_copy, d))
    for h in range(chunks):
        for d in range(2, ways):
            code_copy(d, h).start()
            started.append(functools.partial(code_copy, d, h))
        if h == 0:
            core_copy.start()
            started.append(lambda: core_copy)

    def columns(g):
        return s_hbm.at[:, pl.ds(pl.multiple_of(g * per_group, per_group), per_group)]

    glast = last_group(i, ny, nz)
    shape_copies = []
    if split:
        for d in range(groups):
            g = lax.rem(i + d, groups)
            shape_copies.append(pltpu.make_async_copy(columns(g), shapes.at[g], shape_sem.at[d]))
        shape_copies.append(pltpu.make_async_copy(columns(glast), slast_ref, slast_sem))
    else:
        shape_copies.append(pltpu.make_async_copy(s_hbm, shapes.at[0], shape_sem.at[0]))
    for copy in shape_copies:
        copy.start()

    for load in loads[2:]:
        load.wait()
    k_copy.wait()
    taps_spectrum(first, k_own, len_ref, xs, hs, fh_ref, fl_ref)

    per = slab // BLOCK
    back = [d if d < 2 else (ways // 2 - d // 2) * 2 + d % 2 for d in range(ways)]
    for d in range(2, ways):
        scale_copy(d).wait_recv()
    for d in range(2, ways):
        column = column_of(scales[back[d], 0:1, :].astype(F32), share) * (1 / LEVELS)
        for h in range(chunks):
            steps[d, h] = jnp.broadcast_to(column[h * rows:(h + 1) * rows, :], steps.shape[2:])
    core_copy.wait_recv()

    def hops(h):
        dst, sem = big.at[i, j, h], recv.at[i, j]
        made = []
        for d in range(2, ways):
            made.append((None, remote(mod.at[h, peer(d)], dst, m_send.at[d, h], sem, i, peer(d))))
        for n, tm in enumerate((j, mate)):
            src = mod.at[h, tm]
            for e in range(1, ny):
                made.append((None, remote(src, dst, s_y0.at[e - 1, n, h], sem, z * ny + lax.rem(y + e, ny), tm)))
            if nz > 1:
                made.append((above, remote(src, dst, s_up0.at[n, h], sem, i + ny, tm)))
                made.append((below, remote(src, dst, s_down0.at[n, h], sem, i - ny, tm)))
        made.append((None, remote(mod.at[h, mate], dst, m_send.at[1, h], sem, i, mate)))
        return made

    def chunk(h, carry):
        for d in range(2, ways):
            code_copy(d, h).wait_recv()
        at = pl.ds(pl.multiple_of(h * rows, rows), rows)
        fall[j] = forces[pl.ds(pl.multiple_of(first + h * rows, rows), rows), :]
        fall[mate] = fcore[at, :]
        for d in range(2, ways):
            fall[peer(d)] = codes[back[d], h].astype(jnp.int32).astype(F32) * steps[d, h, :, 0:1]
        blocks = [fall[b // per, :, (b % per) * BLOCK:(b % per + 1) * BLOCK] for b in range(ways * per)]

        def store(b, value):
            mod[h, b // per, :, (b % per) * BLOCK:(b % per + 1) * BLOCK] = value

        filter_rows(blocks, store, hs.at[h], xf, fs, ws, fh_ref, fl_ref, bh_ref, bl_ref)
        for cond, copy in hops(h):
            when(cond, copy.start)
        big[i, j, h] = mod[h, j]
        return carry

    lax.fori_loop(0, chunks, chunk, 0)

    pending = []

    def send(cond, g, q, sem, mode, tm):
        def make():
            return remote(big.at[g, q], big.at[g, q], sem, recv.at[g, q], mode, tm)
        when(cond, lambda: make().start())
        pending.append((cond, make))

    def sent(n):
        for cond, make in pending[:n]:
            when(cond, lambda: make().wait_send())
        del pending[:n]

    def arrived(cond, g, q):
        when(cond, lambda: remote(big.at[g, q], big.at[g, q], own_sem, recv.at[g, q], i, j).wait_recv())

    lane = g_ref.shape[1]
    work = collections.deque()

    def ground(r):
        for part in range(tile // lane):
            at = r * (tile // lane) + part
            column = column_of(g_ref[at:at + 1, :].astype(F32), lane)
            support = lax.broadcasted_iota(jnp.int32, (lane, a_ref.shape[0]), 1).astype(F32)
            hot[part * lane:(part + 1) * lane, :] = (support == column).astype(F32).astype(BF16)
        acc_ref[r * tile:(r + 1) * tile, :] = jnp.dot(hot[...], a_ref[...], preferred_element_type=F32)

    for r in range(dofs // tile):
        work.append((None, functools.partial(ground, r)))

    def product(cond, g):
        if not split:
            return

        def unit(r):
            at = pl.ds(r * tile, tile)
            block = big[g].reshape(per_group, slab)
            acc_ref[at, :] += jnp.dot(shapes[g, at, :], block, preferred_element_type=F32)
        for r in range(dofs // tile):
            work.append((cond, functools.partial(unit, r)))

    def drain(n):
        for _ in range(min(n, len(work))):
            cond, unit = work.popleft()
            when(cond, unit)

    def across(cond, g, q, slot, d):
        for e in range(1, ny):
            send(cond, g, q, s_y.at[slot, e - 1, d], z * ny + lax.rem(y + e, ny), j)

    def up(cond, g, q, slot, d):
        if nz > 1:
            send(both(cond, above), g, q, s_up.at[slot, d], i + ny, j)

    def down(cond, g, q, slot, d):
        if nz > 1:
            send(both(cond, below), g, q, s_down.at[slot, d], i - ny, j)

    partner = z + 1 - 2 * lax.rem(z, 2)

    def own_event(d):
        q = peer(d)
        arrived(None, i, q)
        if d >= 2:
            up(None, i, q, 0, d)
            down(None, i, q, 0, d)
            across(None, i, q, 0, d)

    def event(s, d):
        q = peer(d)
        lower, upper = i - s * ny, i + s * ny
        has_low, has_high = z - s >= 0, z + s <= nz - 1
        spare = relief and s == 1 and d < 2
        if s < nz:
            arrived(has_low, lower, q)
            up(has_low, lower, q, s, d)
            across(both(has_low, z - 1 != partner if spare else None), lower, q, s, d)
            arrived(has_high, upper, q)
            down(has_high, upper, q, s, d)
            across(both(has_high, z + 1 != partner if spare else None), upper, q, nz - 1 + s, d)
        for e in range(1, ny):
            line = lax.rem(y + e, ny)
            if s == 1:
                g = z * ny + line
                arrived(None, g, q)
                if relief and d < 2:
                    send(None, g, q, s_relief.at[d], partner * ny + y, j)
            else:
                arrived(z - s + 1 >= 0, (z - s + 1) * ny + line, q)
                arrived(z + s - 1 <= nz - 1, (z + s - 1) * ny + line, q)

    for copy in shape_copies:
        copy.wait()
    before = 0
    for s in range(1, nz + 1):
        mark = len(pending)
        if s == 2:
            for make in started:
                make().wait_send()

            def hopped(h, carry):
                for cond, copy in hops(h):
                    when(cond, copy.wait_send)
                return carry

            lax.fori_loop(0, chunks, hopped, 0)
        elif s > 2:
            sent(before)
            mark -= before
        for d in range(ways):
            if s == 1 and d > 0:
                if d == 1:
                    own_event(1)
                if d + 1 < ways:
                    own_event(d + 1)
                    if d + 2 == ways:
                        product(None, i)
            event(s, d)
            drain(2 if s == 1 else 3)
        before = mark
        if s < nz:
            product(z - s >= 0, i - s * ny)
            product(z + s <= nz - 1, i + s * ny)
        for e in range(1, ny):
            line = lax.rem(y + e, ny)
            if s == 1:
                g = z * ny + line
                product(g != glast, g)
            else:
                g = (z - s + 1) * ny + line
                product((z - s + 1 >= 0) & (g != glast), g)
                g = (z + s - 1) * ny + line
                product((z + s - 1 <= nz - 1) & (g != glast), g)
    drain(len(work))
    if not split:
        def whole(r, carry):
            at = pl.ds(pl.multiple_of(r * tile, tile), tile)
            block = big[...].reshape(groups * per_group, slab)
            acc_ref[at, :] += jnp.dot(shapes[0, at, :], block, preferred_element_type=F32)
            return carry
        lax.fori_loop(0, dofs // tile, whole, 0)
    sent(len(pending))


def tail_kernel(ny, tile, acc_ref, big, s_ref, o_hbm, out, sem):
    groups, ways, chunks, rows, slab = big.shape
    glast = last_group(lax.axis_index("mode"), ny, groups // ny)
    dofs = acc_ref.shape[0]
    copies = []
    for n in range(dofs // tile):
        at = pl.ds(n * tile, tile)
        total = acc_ref[at, :]
        if s_ref.shape[0] == dofs:
            block = big[glast].reshape(ways * chunks * rows, slab)
            total += jnp.dot(s_ref[at, :], block, preferred_element_type=F32)
        out[at, :] = total.astype(BF16)
        copies.append(pltpu.make_async_copy(out.at[at], o_hbm.at[at], sem.at[n]))
        copies[-1].start()
    for copy in copies:
        copy.wait()


def per_device(support_accel, participation, kernels, lengths, mode_shapes, groups):
    ways, ngroups = lax.axis_size("tm"), lax.axis_size("mode")
    ny, nz = grid_of(ngroups, ways)
    held, taps = kernels.shape
    share = held // ways
    rows = 16 if share % 16 == 0 else share
    chunks = share // rows
    supports, slab = support_accel.shape
    dofs, modes = mode_shapes.shape
    tile = min(512, dofs)
    last_tile = min(256, dofs)
    split = held % 128 == 0 and ny > 1 and dofs > tile
    times = ways * slab
    lanes = -(-share // 128) * 128
    tables = transform_tables()
    hbm = pl.BlockSpec(memory_space=pltpu.HBM)
    vmem = pl.BlockSpec(memory_space=pltpu.VMEM)
    dma = pltpu.SemaphoreType.DMA
    acc, every, shapes = pl.pallas_call(
        functools.partial(main_kernel, ny, tile),
        out_shape=(
            pltpu.VMEM((dofs, slab), F32),
            pltpu.VMEM((ngroups, ways, chunks, rows, slab), BF16),
            pltpu.VMEM((dofs, held) if split else (16, 128), BF16),
        ),
        in_specs=[hbm] * 10,
        out_specs=(vmem, vmem, vmem),
        scratch_shapes=[
            pltpu.VMEM((supports, slab), BF16),
            pltpu.VMEM((held, supports), BF16),
            pltpu.VMEM((1, held), jnp.int32),
            pltpu.VMEM((dofs // 128, 128), jnp.int32),
            *(pltpu.VMEM(table.shape, BF16) for table in tables),
            dma((8,)),
            pltpu.VMEM((share, taps), F32),
            pltpu.VMEM((ngroups, dofs, held) if split else (1, dofs, modes), BF16),
            pltpu.VMEM((held, slab), F32),
            pltpu.VMEM((share, slab), F32),
            pltpu.VMEM((ways, chunks, rows, slab), jnp.int16),
            pltpu.VMEM((ways, chunks, rows, slab), jnp.int16),
            pltpu.VMEM((ways, 16, lanes), BF16),
            pltpu.VMEM((ways, 16, lanes), BF16),
            pltpu.VMEM((ways, chunks, rows, 128), F32),
            pltpu.VMEM((ways, rows, slab), F32),
            pltpu.VMEM((chunks, ways, rows, slab), BF16),
            pltpu.VMEM((chunks, taps // BLOCK * rows, BLOCK), F32),
            pltpu.VMEM((times // BLOCK * rows, BLOCK), F32),
            pltpu.VMEM((times // BLOCK * rows, 2 * BLOCK), F32),
            pltpu.VMEM((chunks, taps // BLOCK * rows, 2 * BLOCK), F32),
            pltpu.VMEM((times // BLOCK * rows, 2 * BLOCK), F32),
            pltpu.VMEM((tile, supports), BF16),
            dma, dma((ngroups,)), dma, dma, dma, dma((ways, chunks)), dma((ways, chunks)), dma((ways,)), dma((ways,)), dma,
            dma((ways, chunks)), dma((ngroups, ways)),
            dma((2, chunks)), dma((2, chunks)), dma((max(ny - 1, 1), 2, chunks)),
            dma((nz, ways)), dma((nz, ways)), dma((2 * nz - 1, max(ny - 1, 1), ways)), dma((2,)),
        ],
        compiler_params=pltpu.CompilerParams(
            collective_id=0, has_side_effects=True, vmem_limit_bytes=40 << 20
        ),
    )(*(pltpu.with_memory_space_constraint(array, pltpu.HBM) for array in (
        support_accel, participation, kernels, lengths.reshape(1, held), mode_shapes,
        groups.reshape(dofs // 128, 128), *map(jnp.asarray, tables),
    )))
    return pl.pallas_call(
        functools.partial(tail_kernel, ny, last_tile),
        out_shape=jax.ShapeDtypeStruct((dofs, slab), BF16),
        in_specs=[vmem, vmem, vmem],
        out_specs=hbm,
        scratch_shapes=[pltpu.VMEM((dofs, slab), BF16), dma((dofs // last_tile,))],
        compiler_params=pltpu.CompilerParams(vmem_limit_bytes=24 << 20),
    )(acc, every, shapes)


def solution(mesh):
    placed = (
        P(None, "tm"),
        P("mode", None),
        P("mode", None),
        P("mode"),
        P("mode", None),
        P("mode"),
    )
    return jax.shard_map(
        per_device, mesh=mesh, in_specs=placed, out_specs=P("mode", "tm"), check_vma=False
    )
```

```python
import collections
import functools

import jax
import jax.numpy as jnp
import numpy as np
from jax import lax
from jax.experimental import pallas as pl
from jax.experimental.pallas import tpu as pltpu
from jax.sharding import PartitionSpec as P

BLOCK = 128
F32 = jnp.float32
BF16 = jnp.bfloat16
MESH = pl.DeviceIdType.MESH


def split_constant(table):
    high = table.astype(BF16)
    low = (table - high.astype(np.float64)).astype(BF16)
    return high, low


def transform_tables():
    angle = np.pi * (np.arange(BLOCK)[:, None] + 0.5) / BLOCK
    time = np.arange(2 * BLOCK)[None, :]
    cos, sin = np.cos(angle * time), np.sin(angle * time)
    forward = np.concatenate([cos[:, :BLOCK], -sin[:, :BLOCK]], axis=0).T
    backward = np.concatenate([cos, -sin], axis=0) / BLOCK
    return split_constant(forward) + split_constant(backward)


def dot3(values, high, low):
    top = values.astype(BF16)
    rest = (values - top.astype(F32)).astype(BF16)
    dot = functools.partial(jnp.dot, preferred_element_type=F32)
    return dot(top, high) + (dot(rest, high) + dot(top, low))


def grid_of(groups, ways):
    ny = max(ways // 2, 1)
    if groups % ny:
        ny = 1
    return ny, groups // ny


def last_group(i, ny, nz):
    z, y = i // ny, lax.rem(i, ny)
    far = jnp.where(2 * z < nz, nz - 1, 0)
    return far * ny + lax.rem(y + 1, ny)


def column_of(row, rows):
    lanes = row.shape[1]
    at = lax.broadcasted_iota(jnp.int32, (rows, lanes), 0) == lax.broadcasted_iota(jnp.int32, (rows, lanes), 1)
    return jnp.sum(jnp.where(at, jnp.broadcast_to(row, (rows, lanes)), 0.0), axis=1, keepdims=True)


def row_of(column, lanes):
    rows = column.shape[0]
    at = lax.broadcasted_iota(jnp.int32, (rows, lanes), 0) == lax.broadcasted_iota(jnp.int32, (rows, lanes), 1)
    return jnp.sum(jnp.where(at, jnp.broadcast_to(column, (rows, lanes)), 0.0), axis=0, keepdims=True)


def taps_spectrum(first, k_own, len_ref, xs, hs, fh_ref, fl_ref):
    share, taps = k_own.shape
    chunks = hs.shape[0]
    rows = share // chunks
    held = len_ref.shape[1]
    picked = lax.broadcasted_iota(jnp.int32, (share, held), 1) == first + lax.broadcasted_iota(jnp.int32, (share, held), 0)
    wide = jnp.broadcast_to(len_ref[...], (share, held)).astype(F32)
    lengths = jnp.sum(jnp.where(picked, wide, 0.0), axis=1, keepdims=True)
    kblocks = taps // BLOCK
    for c in range(kblocks):
        pos = (c * BLOCK + lax.broadcasted_iota(jnp.int32, (share, BLOCK), 1)).astype(F32)
        part = k_own[:, c * BLOCK:(c + 1) * BLOCK]
        part = jnp.where(pos < lengths, part, jnp.zeros_like(part))
        for h in range(chunks):
            xs[h, c * rows:(c + 1) * rows, :] = part[h * rows:(h + 1) * rows, :]
    for h in range(chunks):
        hs[h] = dot3(xs[h, :kblocks * rows, :], fh_ref[...], fl_ref[...])


def filter_rows(blocks, store, hs, xs, fs, ws, fh_ref, fl_ref, bh_ref, bl_ref):
    tblocks = len(blocks)
    rows = blocks[0].shape[0]
    kblocks = hs.shape[0] // rows
    for a in range(tblocks):
        xs[a * rows:(a + 1) * rows, :] = blocks[a]
    fs[...] = dot3(xs[:tblocks * rows, :], fh_ref[...], fl_ref[...])
    for b in range(tblocks):
        re = jnp.zeros((rows, BLOCK), F32)
        im = jnp.zeros((rows, BLOCK), F32)
        for c in range(min(b + 1, kblocks)):
            fr = fs[(b - c) * rows:(b - c + 1) * rows, :BLOCK]
            fi = fs[(b - c) * rows:(b - c + 1) * rows, BLOCK:]
            hr = hs[c * rows:(c + 1) * rows, :BLOCK]
            hi = hs[c * rows:(c + 1) * rows, BLOCK:]
            re = re + (fr * hr - fi * hi)
            im = im + (fr * hi + fi * hr)
        ws[b * rows:(b + 1) * rows, :BLOCK] = re
        ws[b * rows:(b + 1) * rows, BLOCK:] = im
    wide = dot3(ws[...], bh_ref[...], bl_ref[...])
    for b in range(tblocks):
        y = wide[b * rows:(b + 1) * rows, :BLOCK]
        if b:
            y = y + wide[(b - 1) * rows:b * rows, BLOCK:]
        store(b, y.astype(BF16))


def when(cond, body):
    if cond is None:
        body()
    else:
        pl.when(cond)(body)


def both(a, b):
    if a is None:
        return b
    return a if b is None else a & b


LEVELS = 32000.0


def main_kernel(
    ny, tile, a_hbm, p_hbm, k_hbm, len_hbm, s_hbm, g_hbm, fh_hbm, fl_hbm, bh_hbm, bl_hbm,
    acc_ref, big, slast_ref,
    a_ref, p_ref, len_ref, g_ref, fh_ref, fl_ref, bh_ref, bl_ref, in_sem,
    k_own, shapes, forces, fcore, coded, codes, scaled, scales, steps, fall, mod, xs, xf, fs, hs, ws, hot,
    k_sem, shape_sem, slast_sem, core_send, core_recv, code_send, code_recv, scale_send, scale_recv, own_sem,
    m_send, recv, s_up0, s_down0, s_y0, s_up, s_down, s_y, s_relief,
):
    groups, ways, chunks, rows, slab = big.shape
    share = chunks * rows
    dofs = acc_ref.shape[0]
    per_group = ways * share
    nz = groups // ny
    split = shapes.shape[0] == groups
    i, j = lax.axis_index("mode"), lax.axis_index("tm")
    z, y = i // ny, lax.rem(i, ny)
    below, above = z > 0, z < nz - 1
    relief = ny == 2 and nz >= 4 and ways >= 4
    mate = j + 1 - 2 * lax.rem(j, 2)

    def peer(d):
        return lax.rem(j // 2 + d // 2, ways // 2) * 2 + lax.rem(lax.rem(j, 2) + d, 2)

    loads = [
        pltpu.make_async_copy(src, dst, in_sem.at[n])
        for n, (src, dst) in enumerate((
            (a_hbm, a_ref), (p_hbm, p_ref), (len_hbm, len_ref), (fh_hbm, fh_ref), (fl_hbm, fl_ref),
            (bh_hbm, bh_ref), (bl_hbm, bl_ref), (g_hbm, g_ref),
        ))
    ]
    first = j * share
    k_copy = pltpu.make_async_copy(k_hbm.at[pl.ds(pl.multiple_of(first, share), share)], k_own, k_sem)
    for load in loads:
        load.start()
    k_copy.start()

    barrier = pltpu.get_barrier_semaphore()

    def greet(mode, tm):
        pl.semaphore_signal(barrier, inc=1, device_id={"mode": mode, "tm": tm}, device_id_type=MESH)

    for d in range(1, ways):
        greet(i, lax.rem(j + d, ways))
    for tm in (j, mate):
        for e in range(1, ny):
            greet(z * ny + lax.rem(y + e, ny), tm)
        if nz > 1:
            @pl.when(below)
            def _():
                greet(i - ny, tm)

            @pl.when(above)
            def _():
                greet(i + ny, tm)

    loads[0].wait()
    loads[1].wait()
    forces[...] = jnp.dot(p_ref[...], a_ref[...], preferred_element_type=F32)

    def forces_of(q):
        return forces[pl.ds(pl.multiple_of(q * share, share), share), :]

    lanes = scaled.shape[2]
    for d in range(2, ways):
        values = forces_of(peer(d))
        top = jnp.max(jnp.abs(values), axis=1, keepdims=True)
        scale = (top * 1.01 + 1e-30).astype(BF16)
        scaled[d] = jnp.broadcast_to(row_of(scale.astype(F32), lanes), scaled.shape[1:]).astype(BF16)
        values = values * (LEVELS / scale.astype(F32))
        values = jnp.round(values).astype(jnp.int32).astype(jnp.int16)
        for h in range(chunks):
            coded[d, h] = values[h * rows:(h + 1) * rows, :]

    always = ways - 1 + 2 * (ny - 1)
    if nz == 1:
        pl.semaphore_wait(barrier, always)
    else:
        @pl.when(below & above)
        def _():
            pl.semaphore_wait(barrier, always + 4)

        @pl.when(jnp.logical_not(below & above))
        def _():
            pl.semaphore_wait(barrier, always + 2)

    started = []

    def remote(src, dst, send_sem, recv_sem, mode, tm):
        return pltpu.make_async_remote_copy(
            src, dst, send_sem, recv_sem, device_id={"mode": mode, "tm": tm}, device_id_type=MESH,
        )

    def code_copy(d, h):
        return remote(coded.at[d, h], codes.at[d, h], code_send.at[d, h], code_recv.at[d, h], i, peer(d))

    def scale_copy(d):
        return remote(scaled.at[d], scales.at[d], scale_send.at[d], scale_recv.at[d], i, peer(d))

    core_copy = remote(forces.at[pl.ds(pl.multiple_of(mate * share, share), share)], fcore, core_send, core_recv, i, mate)
    for d in range(2, ways):
        scale_copy(d).start()
        started.append(functools.partial(scale_copy, d))
    for h in range(chunks):
        for d in range(2, ways):
            code_copy(d, h).start()
            started.append(functools.partial(code_copy, d, h))
        if h == 0:
            core_copy.start()
            started.append(lambda: core_copy)

    def columns(g):
        return s_hbm.at[:, pl.ds(pl.multiple_of(g * per_group, per_group), per_group)]

    glast = last_group(i, ny, nz)
    shape_copies = []
    if split:
        for d in range(groups):
            g = lax.rem(i + d, groups)
            shape_copies.append(pltpu.make_async_copy(columns(g), shapes.at[g], shape_sem.at[d]))
        shape_copies.append(pltpu.make_async_copy(columns(glast), slast_ref, slast_sem))
    else:
        shape_copies.append(pltpu.make_async_copy(s_hbm, shapes.at[0], shape_sem.at[0]))
    for copy in shape_copies:
        copy.start()

    for load in loads[2:]:
        load.wait()
    k_copy.wait()
    taps_spectrum(first, k_own, len_ref, xs, hs, fh_ref, fl_ref)

    per = slab // BLOCK
    back = [d if d < 2 else (ways // 2 - d // 2) * 2 + d % 2 for d in range(ways)]
    for d in range(2, ways):
        scale_copy(d).wait_recv()
    for d in range(2, ways):
        column = column_of(scales[back[d], 0:1, :].astype(F32), share) * (1 / LEVELS)
        for h in range(chunks):
            steps[d, h] = jnp.broadcast_to(column[h * rows:(h + 1) * rows, :], steps.shape[2:])
    core_copy.wait_recv()

    def hops(h):
        dst, sem = big.at[i, j, h], recv.at[i, j]
        made = []
        for d in range(2, ways):
            made.append((None, remote(mod.at[h, peer(d)], dst, m_send.at[d, h], sem, i, peer(d))))
        for n, tm in enumerate((j, mate)):
            src = mod.at[h, tm]
            for e in range(1, ny):
                made.append((None, remote(src, dst, s_y0.at[e - 1, n, h], sem, z * ny + lax.rem(y + e, ny), tm)))
            if nz > 1:
                made.append((above, remote(src, dst, s_up0.at[n, h], sem, i + ny, tm)))
                made.append((below, remote(src, dst, s_down0.at[n, h], sem, i - ny, tm)))
        made.append((None, remote(mod.at[h, mate], dst, m_send.at[1, h], sem, i, mate)))
        return made

    def chunk(h, carry):
        for d in range(2, ways):
            code_copy(d, h).wait_recv()
        at = pl.ds(pl.multiple_of(h * rows, rows), rows)
        fall[j] = forces[pl.ds(pl.multiple_of(first + h * rows, rows), rows), :]
        fall[mate] = fcore[at, :]
        for d in range(2, ways):
            fall[peer(d)] = codes[back[d], h].astype(jnp.int32).astype(F32) * steps[d, h, :, 0:1]
        blocks = [fall[b // per, :, (b % per) * BLOCK:(b % per + 1) * BLOCK] for b in range(ways * per)]

        def store(b, value):
            mod[h, b // per, :, (b % per) * BLOCK:(b % per + 1) * BLOCK] = value

        filter_rows(blocks, store, hs.at[h], xf, fs, ws, fh_ref, fl_ref, bh_ref, bl_ref)
        for cond, copy in hops(h):
            when(cond, copy.start)
        big[i, j, h] = mod[h, j]
        return carry

    lax.fori_loop(0, chunks, chunk, 0)

    pending = []

    def send(cond, g, q, sem, mode, tm):
        def make():
            return remote(big.at[g, q], big.at[g, q], sem, recv.at[g, q], mode, tm)
        when(cond, lambda: make().start())
        pending.append((cond, make))

    def sent(n):
        for cond, make in pending[:n]:
            when(cond, lambda: make().wait_send())
        del pending[:n]

    def arrived(cond, g, q):
        when(cond, lambda: remote(big.at[g, q], big.at[g, q], own_sem, recv.at[g, q], i, j).wait_recv())

    lane = g_ref.shape[1]
    work = collections.deque()

    def ground(r):
        for part in range(tile // lane):
            at = r * (tile // lane) + part
            column = column_of(g_ref[at:at + 1, :].astype(F32), lane)
            support = lax.broadcasted_iota(jnp.int32, (lane, a_ref.shape[0]), 1).astype(F32)
            hot[part * lane:(part + 1) * lane, :] = (support == column).astype(F32).astype(BF16)
        acc_ref[r * tile:(r + 1) * tile, :] = jnp.dot(hot[...], a_ref[...], preferred_element_type=F32)

    for r in range(dofs // tile):
        work.append((None, functools.partial(ground, r)))

    def product(cond, g):
        if not split:
            return

        def unit(r):
            at = pl.ds(r * tile, tile)
            block = big[g].reshape(per_group, slab)
            acc_ref[at, :] += jnp.dot(shapes[g, at, :], block, preferred_element_type=F32)
        for r in range(dofs // tile):
            work.append((cond, functools.partial(unit, r)))

    def drain(n):
        for _ in range(min(n, len(work))):
            cond, unit = work.popleft()
            when(cond, unit)

    def across(cond, g, q, slot, d):
        for e in range(1, ny):
            send(cond, g, q, s_y.at[slot, e - 1, d], z * ny + lax.rem(y + e, ny), j)

    def up(cond, g, q, slot, d):
        if nz > 1:
            send(both(cond, above), g, q, s_up.at[slot, d], i + ny, j)

    def down(cond, g, q, slot, d):
        if nz > 1:
            send(both(cond, below), g, q, s_down.at[slot, d], i - ny, j)

    def own_event(d):
        q = peer(d)
        arrived(None, i, q)
        if d >= 2:
            up(None, i, q, 0, d)
            down(None, i, q, 0, d)
            across(None, i, q, 0, d)

    def column_event(s, d):
        q = peer(d)
        lower, upper = i - s * ny, i + s * ny
        has_low, has_high = z - s >= 0, z + s <= nz - 1
        far = relief and s == nz - 1 and 2 * d >= ways
        near = relief and s == 1
        arrived(has_low, lower, q)
        up(has_low, lower, q, s, d)
        if not far:
            across(both(has_low, z != 1 if near else None), lower, q, s, d)
        arrived(has_high, upper, q)
        down(has_high, upper, q, s, d)
        if not far:
            across(both(has_high, z != nz - 2 if near else None), upper, q, nz - 1 + s, d)

    def other_event(s, d):
        q = peer(d)
        for e in range(1, ny):
            line = lax.rem(y + e, ny)
            if s == 0:
                g = z * ny + line
                arrived(None, g, q)
                if relief:
                    send(z == 0, g, q, s_relief.at[0, d], i + ny, j)
                    send(z == nz - 1, g, q, s_relief.at[0, d], i - ny, j)
                continue
            lower, upper = (z - s) * ny + line, (z + s) * ny + line
            arrived(z - s >= 0, lower, q)
            arrived(z + s <= nz - 1, upper, q)
            if relief and s == nz - 2 and 2 * d >= ways:
                send(z == nz - 2, lower, q, s_relief.at[1, d], i + ny, j)
                send(z == 1, upper, q, s_relief.at[1, d], i - ny, j)

    def other_products(s):
        for e in range(1, ny):
            line = lax.rem(y + e, ny)
            if s == 0:
                g = z * ny + line
                product(g != glast, g)
                continue
            for level, there in ((z - s, z - s >= 0), (z + s, z + s <= nz - 1)):
                g = level * ny + line
                product(there & (g != glast), g)

    for copy in shape_copies:
        copy.wait()
    for d in range(ways):
        if nz > 1:
            column_event(1, d)
        if d == 0:
            own_event(1)
        if d + 2 < ways:
            own_event(d + 2)
        if d + 3 == ways or (ways == 2 and d == 0):
            product(None, i)
        other_event(0, d)
        drain(2)
    before = len(pending)
    for s in range(2, nz):
        product(z - s + 1 >= 0, i - (s - 1) * ny)
        product(z + s - 1 <= nz - 1, i + (s - 1) * ny)
        other_products(s - 2)
        if s == 2:
            for make in started:
                make().wait_send()

            def hopped(h, carry):
                for cond, copy in hops(h):
                    when(cond, copy.wait_send)
                return carry

            lax.fori_loop(0, chunks, hopped, 0)
        else:
            sent(before)
            before = len(pending)
        for d in range(ways):
            column_event(s, d)
            other_event(s - 1, d)
            drain(3)
    if nz > 1:
        s = nz - 1
        product(z - s >= 0, i - s * ny)
        product(z + s <= nz - 1, i + s * ny)
    other_products(max(nz - 2, 0))
    drain(len(work))
    if nz <= 2:
        for make in started:
            make().wait_send()
        for h in range(chunks):
            for cond, copy in hops(h):
                when(cond, copy.wait_send)
    sent(before)
    if nz > 1:
        for d in range(ways):
            other_event(nz - 1, d)
        other_products(nz - 1)
    drain(len(work))
    if not split:
        def whole(r, carry):
            at = pl.ds(pl.multiple_of(r * tile, tile), tile)
            block = big[...].reshape(groups * per_group, slab)
            acc_ref[at, :] += jnp.dot(shapes[0, at, :], block, preferred_element_type=F32)
            return carry
        lax.fori_loop(0, dofs // tile, whole, 0)
    sent(len(pending))


def tail_kernel(ny, tile, acc_ref, big, s_ref, o_hbm, out, sem):
    groups, ways, chunks, rows, slab = big.shape
    glast = last_group(lax.axis_index("mode"), ny, groups // ny)
    dofs = acc_ref.shape[0]
    copies = []
    for n in range(dofs // tile):
        at = pl.ds(n * tile, tile)
        total = acc_ref[at, :]
        if s_ref.shape[0] == dofs:
            block = big[glast].reshape(ways * chunks * rows, slab)
            total += jnp.dot(s_ref[at, :], block, preferred_element_type=F32)
        out[at, :] = total.astype(BF16)
        copies.append(pltpu.make_async_copy(out.at[at], o_hbm.at[at], sem.at[n]))
        copies[-1].start()
    for copy in copies:
        copy.wait()


def per_device(support_accel, participation, kernels, lengths, mode_shapes, groups):
    ways, ngroups = lax.axis_size("tm"), lax.axis_size("mode")
    ny, nz = grid_of(ngroups, ways)
    held, taps = kernels.shape
    share = held // ways
    rows = 16 if share % 16 == 0 else share
    chunks = share // rows
    supports, slab = support_accel.shape
    dofs, modes = mode_shapes.shape
    tile = min(512, dofs)
    last_tile = min(256, dofs)
    split = held % 128 == 0 and ny > 1 and dofs > tile
    times = ways * slab
    lanes = -(-share // 128) * 128
    tables = transform_tables()
    hbm = pl.BlockSpec(memory_space=pltpu.HBM)
    vmem = pl.BlockSpec(memory_space=pltpu.VMEM)
    dma = pltpu.SemaphoreType.DMA
    acc, every, shapes = pl.pallas_call(
        functools.partial(main_kernel, ny, tile),
        out_shape=(
            pltpu.VMEM((dofs, slab), F32),
            pltpu.VMEM((ngroups, ways, chunks, rows, slab), BF16),
            pltpu.VMEM((dofs, held) if split else (16, 128), BF16),
        ),
        in_specs=[hbm] * 10,
        out_specs=(vmem, vmem, vmem),
        scratch_shapes=[
            pltpu.VMEM((supports, slab), BF16),
            pltpu.VMEM((held, supports), BF16),
            pltpu.VMEM((1, held), jnp.int32),
            pltpu.VMEM((dofs // 128, 128), jnp.int32),
            *(pltpu.VMEM(table.shape, BF16) for table in tables),
            dma((8,)),
            pltpu.VMEM((share, taps), F32),
            pltpu.VMEM((ngroups, dofs, held) if split else (1, dofs, modes), BF16),
            pltpu.VMEM((held, slab), F32),
            pltpu.VMEM((share, slab), F32),
            pltpu.VMEM((ways, chunks, rows, slab), jnp.int16),
            pltpu.VMEM((ways, chunks, rows, slab), jnp.int16),
            pltpu.VMEM((ways, 16, lanes), BF16),
            pltpu.VMEM((ways, 16, lanes), BF16),
            pltpu.VMEM((ways, chunks, rows, 128), F32),
            pltpu.VMEM((ways, rows, slab), F32),
            pltpu.VMEM((chunks, ways, rows, slab), BF16),
            pltpu.VMEM((chunks, taps // BLOCK * rows, BLOCK), F32),
            pltpu.VMEM((times // BLOCK * rows, BLOCK), F32),
            pltpu.VMEM((times // BLOCK * rows, 2 * BLOCK), F32),
            pltpu.VMEM((chunks, taps // BLOCK * rows, 2 * BLOCK), F32),
            pltpu.VMEM((times // BLOCK * rows, 2 * BLOCK), F32),
            pltpu.VMEM((tile, supports), BF16),
            dma, dma((ngroups,)), dma, dma, dma, dma((ways, chunks)), dma((ways, chunks)), dma((ways,)), dma((ways,)), dma,
            dma((ways, chunks)), dma((ngroups, ways)),
            dma((2, chunks)), dma((2, chunks)), dma((max(ny - 1, 1), 2, chunks)),
            dma((nz, ways)), dma((nz, ways)), dma((2 * nz - 1, max(ny - 1, 1), ways)), dma((2, ways)),
        ],
        compiler_params=pltpu.CompilerParams(
            collective_id=0, has_side_effects=True, vmem_limit_bytes=40 << 20
        ),
    )(*(pltpu.with_memory_space_constraint(array, pltpu.HBM) for array in (
        support_accel, participation, kernels, lengths.reshape(1, held), mode_shapes,
        groups.reshape(dofs // 128, 128), *map(jnp.asarray, tables),
    )))
    return pl.pallas_call(
        functools.partial(tail_kernel, ny, last_tile),
        out_shape=jax.ShapeDtypeStruct((dofs, slab), BF16),
        in_specs=[vmem, vmem, vmem],
        out_specs=hbm,
        scratch_shapes=[pltpu.VMEM((dofs, slab), BF16), dma((dofs // last_tile,))],
        compiler_params=pltpu.CompilerParams(vmem_limit_bytes=24 << 20),
    )(acc, every, shapes)


def solution(mesh):
    placed = (
        P(None, "tm"),
        P("mode", None),
        P("mode", None),
        P("mode"),
        P("mode", None),
        P("mode"),
    )
    return jax.shard_map(
        per_device, mesh=mesh, in_specs=placed, out_specs=P("mode", "tm"), check_vma=False
    )
```

```python
import collections
import functools

import jax
import jax.numpy as jnp
import numpy as np
from jax import lax
from jax.experimental import pallas as pl
from jax.experimental.pallas import tpu as pltpu
from jax.sharding import PartitionSpec as P

BLOCK = 128
F32 = jnp.float32
BF16 = jnp.bfloat16
MESH = pl.DeviceIdType.MESH


def split_constant(table):
    high = table.astype(BF16)
    low = (table - high.astype(np.float64)).astype(BF16)
    return high, low


def transform_tables():
    angle = np.pi * (np.arange(BLOCK)[:, None] + 0.5) / BLOCK
    time = np.arange(2 * BLOCK)[None, :]
    cos, sin = np.cos(angle * time), np.sin(angle * time)
    forward = np.concatenate([cos[:, :BLOCK], -sin[:, :BLOCK]], axis=0).T
    backward = np.concatenate([cos, -sin], axis=0) / BLOCK
    tables = []
    for table in (forward, backward):
        high, low = split_constant(table)
        tables.append(np.concatenate([high, high, low], axis=0))
    return tables


def dot3(values, table):
    top = values.astype(BF16)
    rest = (values - top.astype(F32)).astype(BF16)
    return jnp.dot(jnp.concatenate([top, rest, top], axis=1), table, preferred_element_type=F32)


def grid_of(groups, ways):
    ny = max(ways // 2, 1)
    if groups % ny:
        ny = 1
    return ny, groups // ny


def last_group(i, ny, nz):
    z, y = i // ny, lax.rem(i, ny)
    far = jnp.where(2 * z < nz, nz - 1, 0)
    return far * ny + lax.rem(y + 1, ny)


def column_of(row, rows):
    lanes = row.shape[1]
    at = lax.broadcasted_iota(jnp.int32, (rows, lanes), 0) == lax.broadcasted_iota(jnp.int32, (rows, lanes), 1)
    return jnp.sum(jnp.where(at, jnp.broadcast_to(row, (rows, lanes)), 0.0), axis=1, keepdims=True)


def row_of(column, lanes):
    rows = column.shape[0]
    at = lax.broadcasted_iota(jnp.int32, (rows, lanes), 0) == lax.broadcasted_iota(jnp.int32, (rows, lanes), 1)
    return jnp.sum(jnp.where(at, jnp.broadcast_to(column, (rows, lanes)), 0.0), axis=0, keepdims=True)


def taps_spectrum(first, k_own, len_ref, xs, hs, f_table):
    share, taps = k_own.shape
    chunks = hs.shape[0]
    rows = share // chunks
    held = len_ref.shape[1]
    picked = lax.broadcasted_iota(jnp.int32, (share, held), 1) == first + lax.broadcasted_iota(jnp.int32, (share, held), 0)
    wide = jnp.broadcast_to(len_ref[...], (share, held)).astype(F32)
    lengths = jnp.sum(jnp.where(picked, wide, 0.0), axis=1, keepdims=True)
    kblocks = taps // BLOCK
    for c in range(kblocks):
        pos = (c * BLOCK + lax.broadcasted_iota(jnp.int32, (share, BLOCK), 1)).astype(F32)
        part = k_own[:, c * BLOCK:(c + 1) * BLOCK]
        part = jnp.where(pos < lengths, part, jnp.zeros_like(part))
        for h in range(chunks):
            xs[h, c * rows:(c + 1) * rows, :] = part[h * rows:(h + 1) * rows, :]
    for h in range(chunks):
        hs[h] = dot3(xs[h, :kblocks * rows, :], f_table[...])


def filter_rows(blocks, store, hs, xs, fs, ws, f_table, b_table):
    tblocks = len(blocks)
    rows = blocks[0].shape[0]
    kblocks = hs.shape[0] // rows
    for a in range(tblocks):
        xs[a * rows:(a + 1) * rows, :] = blocks[a]
    fs[...] = dot3(xs[:tblocks * rows, :], f_table[...])
    for b in range(tblocks):
        re = jnp.zeros((rows, BLOCK), F32)
        im = jnp.zeros((rows, BLOCK), F32)
        for c in range(min(b + 1, kblocks)):
            fr = fs[(b - c) * rows:(b - c + 1) * rows, :BLOCK]
            fi = fs[(b - c) * rows:(b - c + 1) * rows, BLOCK:]
            hr = hs[c * rows:(c + 1) * rows, :BLOCK]
            hi = hs[c * rows:(c + 1) * rows, BLOCK:]
            re = re + (fr * hr - fi * hi)
            im = im + (fr * hi + fi * hr)
        ws[b * rows:(b + 1) * rows, :BLOCK] = re
        ws[b * rows:(b + 1) * rows, BLOCK:] = im
    wide = dot3(ws[...], b_table[...])
    for b in range(tblocks):
        y = wide[b * rows:(b + 1) * rows, :BLOCK]
        if b:
            y = y + wide[(b - 1) * rows:b * rows, BLOCK:]
        store(b, y.astype(BF16))


def when(cond, body):
    if cond is None:
        body()
    else:
        pl.when(cond)(body)


def both(a, b):
    if a is None:
        return b
    return a if b is None else a & b


LEVELS = 32000.0


def main_kernel(
    ny, tile, a_hbm, p_hbm, k_hbm, len_hbm, s_hbm, g_hbm, ft_hbm, bt_hbm,
    acc_ref, big, slast_ref,
    a_ref, p_ref, len_ref, g_ref, f_table, b_table, in_sem,
    k_own, shapes, forces, fcore, coded, codes, scaled, scales, steps, fall, mod, xs, xf, fs, hs, ws, hot,
    k_sem, shape_sem, slast_sem, core_send, core_recv, code_send, code_recv, scale_send, scale_recv, own_sem,
    m_send, recv, s_up0, s_down0, s_y0, s_up, s_down, s_y, s_relief,
):
    groups, ways, chunks, rows, slab = big.shape
    share = chunks * rows
    halves = recv.shape[2]
    part = chunks // halves
    dofs = acc_ref.shape[0]
    per_group = ways * share
    nz = groups // ny
    split = shapes.shape[0] == groups
    i, j = lax.axis_index("mode"), lax.axis_index("tm")
    z, y = i // ny, lax.rem(i, ny)
    below, above = z > 0, z < nz - 1
    relief = ny == 2 and nz >= 4 and ways >= 4
    mate = j + 1 - 2 * lax.rem(j, 2)

    def peer(d):
        return lax.rem(j // 2 + d // 2, ways // 2) * 2 + lax.rem(lax.rem(j, 2) + d, 2)

    loads = [
        pltpu.make_async_copy(src, dst, in_sem.at[n])
        for n, (src, dst) in enumerate((
            (a_hbm, a_ref), (p_hbm, p_ref), (len_hbm, len_ref), (ft_hbm, f_table), (bt_hbm, b_table), (g_hbm, g_ref),
        ))
    ]
    first = j * share
    k_copy = pltpu.make_async_copy(k_hbm.at[pl.ds(pl.multiple_of(first, share), share)], k_own, k_sem)
    for load in loads:
        load.start()
    k_copy.start()

    barrier = pltpu.get_barrier_semaphore()

    def greet(mode, tm):
        pl.semaphore_signal(barrier, inc=1, device_id={"mode": mode, "tm": tm}, device_id_type=MESH)

    for d in range(1, ways):
        greet(i, lax.rem(j + d, ways))
    for tm in (j, mate):
        for e in range(1, ny):
            greet(z * ny + lax.rem(y + e, ny), tm)
        if nz > 1:
            @pl.when(below)
            def _():
                greet(i - ny, tm)

            @pl.when(above)
            def _():
                greet(i + ny, tm)

    loads[0].wait()
    loads[1].wait()
    forces[...] = jnp.dot(p_ref[...], a_ref[...], preferred_element_type=F32)

    def forces_of(q):
        return forces[pl.ds(pl.multiple_of(q * share, share), share), :]

    lanes = scaled.shape[2]
    for d in range(2, ways):
        values = forces_of(peer(d))
        top = jnp.max(jnp.abs(values), axis=1, keepdims=True)
        scale = (top * 1.01 + 1e-30).astype(BF16)
        scaled[d] = jnp.broadcast_to(row_of(scale.astype(F32), lanes), scaled.shape[1:]).astype(BF16)
        values = values * (LEVELS / scale.astype(F32))
        values = jnp.round(values).astype(jnp.int32).astype(jnp.int16)
        for h in range(chunks):
            coded[d, h] = values[h * rows:(h + 1) * rows, :]

    always = ways - 1 + 2 * (ny - 1)
    if nz == 1:
        pl.semaphore_wait(barrier, always)
    else:
        @pl.when(below & above)
        def _():
            pl.semaphore_wait(barrier, always + 4)

        @pl.when(jnp.logical_not(below & above))
        def _():
            pl.semaphore_wait(barrier, always + 2)

    started = []

    def remote(src, dst, send_sem, recv_sem, mode, tm):
        return pltpu.make_async_remote_copy(
            src, dst, send_sem, recv_sem, device_id={"mode": mode, "tm": tm}, device_id_type=MESH,
        )

    def code_copy(d, h):
        return remote(coded.at[d, h], codes.at[d, h], code_send.at[d, h], code_recv.at[d, h], i, peer(d))

    def scale_copy(d):
        return remote(scaled.at[d], scales.at[d], scale_send.at[d], scale_recv.at[d], i, peer(d))

    core_copy = remote(forces.at[pl.ds(pl.multiple_of(mate * share, share), share)], fcore, core_send, core_recv, i, mate)
    for d in range(2, ways):
        scale_copy(d).start()
        started.append(functools.partial(scale_copy, d))
    for h in range(chunks):
        for d in range(2, ways):
            code_copy(d, h).start()
            started.append(functools.partial(code_copy, d, h))
        if h == 0:
            core_copy.start()
            started.append(lambda: core_copy)

    def columns(g):
        return s_hbm.at[:, pl.ds(pl.multiple_of(g * per_group, per_group), per_group)]

    glast = last_group(i, ny, nz)
    shape_copies = []
    if split:
        for d in range(groups):
            g = lax.rem(i + d, groups)
            shape_copies.append(pltpu.make_async_copy(columns(g), shapes.at[g], shape_sem.at[d]))
        shape_copies.append(pltpu.make_async_copy(columns(glast), slast_ref, slast_sem))
    else:
        shape_copies.append(pltpu.make_async_copy(s_hbm, shapes.at[0], shape_sem.at[0]))
    for copy in shape_copies:
        copy.start()

    for load in loads[2:]:
        load.wait()
    k_copy.wait()
    taps_spectrum(first, k_own, len_ref, xs, hs, f_table)

    per = slab // BLOCK
    back = [d if d < 2 else (ways // 2 - d // 2) * 2 + d % 2 for d in range(ways)]
    for d in range(2, ways):
        scale_copy(d).wait_recv()
    for d in range(2, ways):
        column = column_of(scales[back[d], 0:1, :].astype(F32), share) * (1 / LEVELS)
        for h in range(chunks):
            steps[d, h] = jnp.broadcast_to(column[h * rows:(h + 1) * rows, :], steps.shape[2:])
    core_copy.wait_recv()

    def hops(h):
        dst, sem = big.at[i, j, h], recv.at[i, j, h // part]
        made = []
        for d in range(2, ways):
            made.append((None, remote(mod.at[h, peer(d)], dst, m_send.at[d, h], sem, i, peer(d))))
        for n, tm in enumerate((j, mate)):
            src = mod.at[h, tm]
            for e in range(1, ny):
                made.append((None, remote(src, dst, s_y0.at[e - 1, n, h], sem, z * ny + lax.rem(y + e, ny), tm)))
            if nz > 1:
                made.append((above, remote(src, dst, s_up0.at[n, h], sem, i + ny, tm)))
                made.append((below, remote(src, dst, s_down0.at[n, h], sem, i - ny, tm)))
        made.append((None, remote(mod.at[h, mate], dst, m_send.at[1, h], sem, i, mate)))
        return made

    def chunk(h, carry):
        for d in range(2, ways):
            code_copy(d, h).wait_recv()
        at = pl.ds(pl.multiple_of(h * rows, rows), rows)
        fall[j] = forces[pl.ds(pl.multiple_of(first + h * rows, rows), rows), :]
        fall[mate] = fcore[at, :]
        for d in range(2, ways):
            fall[peer(d)] = codes[back[d], h].astype(jnp.int32).astype(F32) * steps[d, h, :, 0:1]
        blocks = [fall[b // per, :, (b % per) * BLOCK:(b % per + 1) * BLOCK] for b in range(ways * per)]

        def store(b, value):
            mod[h, b // per, :, (b % per) * BLOCK:(b % per + 1) * BLOCK] = value

        filter_rows(blocks, store, hs.at[h], xf, fs, ws, f_table, b_table)
        for cond, copy in hops(h):
            when(cond, copy.start)
        big[i, j, h] = mod[h, j]
        return carry

    lax.fori_loop(0, chunks, chunk, 0)

    pending = []

    def half(g, q, k):
        return big.at[g, q, pl.ds(k * part, part)]

    def send(cond, g, q, k, sem, mode, tm):
        def make():
            return remote(half(g, q, k), half(g, q, k), sem.at[k], recv.at[g, q, k], mode, tm)
        when(cond, lambda: make().start())
        pending.append((cond, make))

    def sent(n):
        for cond, make in pending[:n]:
            when(cond, lambda: make().wait_send())
        del pending[:n]

    def arrived(cond, g, q, k):
        when(cond, lambda: remote(half(g, q, k), half(g, q, k), own_sem, recv.at[g, q, k], i, j).wait_recv())

    lane = g_ref.shape[1]
    work = collections.deque()

    def ground(r):
        for part in range(tile // lane):
            at = r * (tile // lane) + part
            column = column_of(g_ref[at:at + 1, :].astype(F32), lane)
            support = lax.broadcasted_iota(jnp.int32, (lane, a_ref.shape[0]), 1).astype(F32)
            hot[part * lane:(part + 1) * lane, :] = (support == column).astype(F32).astype(BF16)
        acc_ref[r * tile:(r + 1) * tile, :] = jnp.dot(hot[...], a_ref[...], preferred_element_type=F32)

    for r in range(dofs // tile):
        work.append((None, functools.partial(ground, r)))

    def product(cond, g):
        if not split:
            return

        def unit(r):
            at = pl.ds(r * tile, tile)
            block = big[g].reshape(per_group, slab)
            acc_ref[at, :] += jnp.dot(shapes[g, at, :], block, preferred_element_type=F32)
        for r in range(dofs // tile):
            work.append((cond, functools.partial(unit, r)))

    def drain(n):
        for _ in range(min(n, len(work))):
            cond, unit = work.popleft()
            when(cond, unit)

    def across(cond, g, q, k, slot, d):
        for e in range(1, ny):
            send(cond, g, q, k, s_y.at[slot, e - 1, d], z * ny + lax.rem(y + e, ny), j)

    def up(cond, g, q, k, slot, d):
        if nz > 1:
            send(both(cond, above), g, q, k, s_up.at[slot, d], i + ny, j)

    def down(cond, g, q, k, slot, d):
        if nz > 1:
            send(both(cond, below), g, q, k, s_down.at[slot, d], i - ny, j)

    def own_event(d, k):
        q = peer(d)
        arrived(None, i, q, k)
        if d >= 2:
            up(None, i, q, k, 0, d)
            down(None, i, q, k, 0, d)
            across(None, i, q, k, 0, d)

    def column_event(s, d, k):
        q = peer(d)
        lower, upper = i - s * ny, i + s * ny
        has_low, has_high = z - s >= 0, z + s <= nz - 1
        far = relief and s == nz - 1 and 2 * d >= ways
        near = relief and s == 1
        arrived(has_low, lower, q, k)
        up(has_low, lower, q, k, s, d)
        if not far:
            across(both(has_low, z != 1 if near else None), lower, q, k, s, d)
        arrived(has_high, upper, q, k)
        down(has_high, upper, q, k, s, d)
        if not far:
            across(both(has_high, z != nz - 2 if near else None), upper, q, k, nz - 1 + s, d)

    def other_event(s, d, k):
        q = peer(d)
        for e in range(1, ny):
            line = lax.rem(y + e, ny)
            if s == 0:
                g = z * ny + line
                arrived(None, g, q, k)
                if relief:
                    send(z == 0, g, q, k, s_relief.at[0, d], i + ny, j)
                    send(z == nz - 1, g, q, k, s_relief.at[0, d], i - ny, j)
                continue
            lower, upper = (z - s) * ny + line, (z + s) * ny + line
            arrived(z - s >= 0, lower, q, k)
            arrived(z + s <= nz - 1, upper, q, k)
            if relief and s == nz - 2 and 2 * d >= ways:
                send(z == nz - 2, lower, q, k, s_relief.at[1, d], i + ny, j)
                send(z == 1, upper, q, k, s_relief.at[1, d], i - ny, j)

    def other_products(s):
        for e in range(1, ny):
            line = lax.rem(y + e, ny)
            if s == 0:
                g = z * ny + line
                product(g != glast, g)
                continue
            for level, there in ((z - s, z - s >= 0), (z + s, z + s <= nz - 1)):
                g = level * ny + line
                product(there & (g != glast), g)

    for copy in shape_copies:
        copy.wait()
    near_ones, far_ones = range(min(2, ways)), range(2, ways)
    for k in range(halves):
        for d in near_ones:
            if nz > 1:
                column_event(1, d, k)
            for f in far_ones:
                if f % 2 == d:
                    own_event(f, k)
        own_event(1, k)
        for d in near_ones:
            other_event(0, d, k)
        drain(2)
    product(None, i)
    for k in range(halves):
        for d in far_ones:
            if nz > 1:
                column_event(1, d, k)
            other_event(0, d, k)
            drain(1)
    before = len(pending)
    for s in range(2, nz):
        product(z - s + 1 >= 0, i - (s - 1) * ny)
        product(z + s - 1 <= nz - 1, i + (s - 1) * ny)
        other_products(s - 2)
        if s == 2:
            for make in started:
                make().wait_send()

            def hopped(h, carry):
                for cond, copy in hops(h):
                    when(cond, copy.wait_send)
                return carry

            lax.fori_loop(0, chunks, hopped, 0)
        else:
            sent(before)
            before = len(pending)
        for some in (near_ones, far_ones):
            for k in range(halves):
                for d in some:
                    column_event(s, d, k)
                    other_event(s - 1, d, k)
                    drain(2)
    if nz > 1:
        s = nz - 1
        product(z - s >= 0, i - s * ny)
        product(z + s <= nz - 1, i + s * ny)
    other_products(max(nz - 2, 0))
    drain(len(work))
    if nz <= 2:
        for make in started:
            make().wait_send()
        for h in range(chunks):
            for cond, copy in hops(h):
                when(cond, copy.wait_send)
    sent(before)
    if nz > 1:
        for d in range(ways):
            for k in range(halves):
                other_event(nz - 1, d, k)
        other_products(nz - 1)
    drain(len(work))
    if not split:
        def whole(r, carry):
            at = pl.ds(pl.multiple_of(r * tile, tile), tile)
            block = big[...].reshape(groups * per_group, slab)
            acc_ref[at, :] += jnp.dot(shapes[0, at, :], block, preferred_element_type=F32)
            return carry
        lax.fori_loop(0, dofs // tile, whole, 0)
    sent(len(pending))


def tail_kernel(ny, tile, acc_ref, big, s_ref, o_hbm, out, sem):
    groups, ways, chunks, rows, slab = big.shape
    glast = last_group(lax.axis_index("mode"), ny, groups // ny)
    dofs = acc_ref.shape[0]
    copies = []
    for n in range(dofs // tile):
        at = pl.ds(n * tile, tile)
        total = acc_ref[at, :]
        if s_ref.shape[0] == dofs:
            block = big[glast].reshape(ways * chunks * rows, slab)
            total += jnp.dot(s_ref[at, :], block, preferred_element_type=F32)
        out[at, :] = total.astype(BF16)
        copies.append(pltpu.make_async_copy(out.at[at], o_hbm.at[at], sem.at[n]))
        copies[-1].start()
    for copy in copies:
        copy.wait()


def per_device(support_accel, participation, kernels, lengths, mode_shapes, groups):
    ways, ngroups = lax.axis_size("tm"), lax.axis_size("mode")
    ny, nz = grid_of(ngroups, ways)
    held, taps = kernels.shape
    share = held // ways
    rows = 16 if share % 16 == 0 else share
    chunks = share // rows
    halves = 2 if chunks % 2 == 0 else 1
    supports, slab = support_accel.shape
    dofs, modes = mode_shapes.shape
    tile = min(512, dofs)
    last_tile = min(256, dofs)
    split = held % 128 == 0 and ny > 1 and dofs > tile
    times = ways * slab
    lanes = -(-share // 128) * 128
    tables = transform_tables()
    hbm = pl.BlockSpec(memory_space=pltpu.HBM)
    vmem = pl.BlockSpec(memory_space=pltpu.VMEM)
    dma = pltpu.SemaphoreType.DMA
    acc, every, shapes = pl.pallas_call(
        functools.partial(main_kernel, ny, tile),
        out_shape=(
            pltpu.VMEM((dofs, slab), F32),
            pltpu.VMEM((ngroups, ways, chunks, rows, slab), BF16),
            pltpu.VMEM((dofs, held) if split else (16, 128), BF16),
        ),
        in_specs=[hbm] * 8,
        out_specs=(vmem, vmem, vmem),
        scratch_shapes=[
            pltpu.VMEM((supports, slab), BF16),
            pltpu.VMEM((held, supports), BF16),
            pltpu.VMEM((1, held), jnp.int32),
            pltpu.VMEM((dofs // 128, 128), jnp.int32),
            *(pltpu.VMEM(table.shape, BF16) for table in tables),
            dma((6,)),
            pltpu.VMEM((share, taps), F32),
            pltpu.VMEM((ngroups, dofs, held) if split else (1, dofs, modes), BF16),
            pltpu.VMEM((held, slab), F32),
            pltpu.VMEM((share, slab), F32),
            pltpu.VMEM((ways, chunks, rows, slab), jnp.int16),
            pltpu.VMEM((ways, chunks, rows, slab), jnp.int16),
            pltpu.VMEM((ways, 16, lanes), BF16),
            pltpu.VMEM((ways, 16, lanes), BF16),
            pltpu.VMEM((ways, chunks, rows, 128), F32),
            pltpu.VMEM((ways, rows, slab), F32),
            pltpu.VMEM((chunks, ways, rows, slab), BF16),
            pltpu.VMEM((chunks, taps // BLOCK * rows, BLOCK), F32),
            pltpu.VMEM((times // BLOCK * rows, BLOCK), F32),
            pltpu.VMEM((times // BLOCK * rows, 2 * BLOCK), F32),
            pltpu.VMEM((chunks, taps // BLOCK * rows, 2 * BLOCK), F32),
            pltpu.VMEM((times // BLOCK * rows, 2 * BLOCK), F32),
            pltpu.VMEM((tile, supports), BF16),
            dma, dma((ngroups,)), dma, dma, dma, dma((ways, chunks)), dma((ways, chunks)), dma((ways,)), dma((ways,)), dma,
            dma((ways, chunks)), dma((ngroups, ways, halves)),
            dma((2, chunks)), dma((2, chunks)), dma((max(ny - 1, 1), 2, chunks)),
            dma((nz, ways, halves)), dma((nz, ways, halves)), dma((2 * nz - 1, max(ny - 1, 1), ways, halves)),
            dma((2, ways, halves)),
        ],
        compiler_params=pltpu.CompilerParams(
            collective_id=0, has_side_effects=True, vmem_limit_bytes=40 << 20
        ),
    )(*(pltpu.with_memory_space_constraint(array, pltpu.HBM) for array in (
        support_accel, participation, kernels, lengths.reshape(1, held), mode_shapes,
        groups.reshape(dofs // 128, 128), *map(jnp.asarray, tables),
    )))
    return pl.pallas_call(
        functools.partial(tail_kernel, ny, last_tile),
        out_shape=jax.ShapeDtypeStruct((dofs, slab), BF16),
        in_specs=[vmem, vmem, vmem],
        out_specs=hbm,
        scratch_shapes=[pltpu.VMEM((dofs, slab), BF16), dma((dofs // last_tile,))],
        compiler_params=pltpu.CompilerParams(vmem_limit_bytes=24 << 20),
    )(acc, every, shapes)


def solution(mesh):
    placed = (
        P(None, "tm"),
        P("mode", None),
        P("mode", None),
        P("mode"),
        P("mode", None),
        P("mode"),
    )
    return jax.shard_map(
        per_device, mesh=mesh, in_specs=placed, out_specs=P("mode", "tm"), check_vma=False
    )
```

```python
import collections
import functools

import jax
import jax.numpy as jnp
import numpy as np
from jax import lax
from jax.experimental import pallas as pl
from jax.experimental.pallas import tpu as pltpu
from jax.sharding import PartitionSpec as P

BLOCK = 128
F32 = jnp.float32
BF16 = jnp.bfloat16
MESH = pl.DeviceIdType.MESH


def split_constant(table):
    high = table.astype(BF16)
    low = (table - high.astype(np.float64)).astype(BF16)
    return high, low


def transform_tables():
    angle = np.pi * (np.arange(BLOCK)[:, None] + 0.5) / BLOCK
    time = np.arange(2 * BLOCK)[None, :]
    cos, sin = np.cos(angle * time), np.sin(angle * time)
    forward = np.concatenate([cos[:, :BLOCK], -sin[:, :BLOCK]], axis=0).T
    backward = np.concatenate([cos, -sin], axis=0) / BLOCK
    tables = []
    for table in (forward, backward):
        high, low = split_constant(table)
        tables.append(np.concatenate([high, high, low], axis=0))
    return tables


def dot3(values, table):
    top = values.astype(BF16)
    rest = (values - top.astype(F32)).astype(BF16)
    return jnp.dot(jnp.concatenate([top, rest, top], axis=1), table, preferred_element_type=F32)


def grid_of(groups, ways):
    ny = max(ways // 2, 1)
    if groups % ny:
        ny = 1
    return ny, groups // ny


def last_group(i, ny, nz):
    z, y = i // ny, lax.rem(i, ny)
    far = jnp.where(2 * z < nz, nz - 1, 0)
    return far * ny + lax.rem(y + 1, ny)


def column_of(row, rows):
    lanes = row.shape[1]
    at = lax.broadcasted_iota(jnp.int32, (rows, lanes), 0) == lax.broadcasted_iota(jnp.int32, (rows, lanes), 1)
    return jnp.sum(jnp.where(at, jnp.broadcast_to(row, (rows, lanes)), 0.0), axis=1, keepdims=True)


def row_of(column, lanes):
    rows = column.shape[0]
    at = lax.broadcasted_iota(jnp.int32, (rows, lanes), 0) == lax.broadcasted_iota(jnp.int32, (rows, lanes), 1)
    return jnp.sum(jnp.where(at, jnp.broadcast_to(column, (rows, lanes)), 0.0), axis=0, keepdims=True)


def taps_spectrum(first, k_own, len_ref, xs, hs, f_table):
    share, taps = k_own.shape
    chunks = hs.shape[0]
    rows = share // chunks
    held = len_ref.shape[1]
    picked = lax.broadcasted_iota(jnp.int32, (share, held), 1) == first + lax.broadcasted_iota(jnp.int32, (share, held), 0)
    wide = jnp.broadcast_to(len_ref[...], (share, held)).astype(F32)
    lengths = jnp.sum(jnp.where(picked, wide, 0.0), axis=1, keepdims=True)
    kblocks = taps // BLOCK
    for c in range(kblocks):
        pos = (c * BLOCK + lax.broadcasted_iota(jnp.int32, (share, BLOCK), 1)).astype(F32)
        part = k_own[:, c * BLOCK:(c + 1) * BLOCK]
        part = jnp.where(pos < lengths, part, jnp.zeros_like(part))
        for h in range(chunks):
            xs[h, c * rows:(c + 1) * rows, :] = part[h * rows:(h + 1) * rows, :]
    for h in range(chunks):
        hs[h] = dot3(xs[h, :kblocks * rows, :], f_table[...])


def filter_rows(blocks, store, hs, xs, fs, ws, f_table, b_table):
    tblocks = len(blocks)
    rows = blocks[0].shape[0]
    kblocks = hs.shape[0] // rows
    for a in range(tblocks):
        xs[a * rows:(a + 1) * rows, :] = blocks[a]
    fs[...] = dot3(xs[:tblocks * rows, :], f_table[...])
    for b in range(tblocks):
        re = jnp.zeros((rows, BLOCK), F32)
        im = jnp.zeros((rows, BLOCK), F32)
        for c in range(min(b + 1, kblocks)):
            fr = fs[(b - c) * rows:(b - c + 1) * rows, :BLOCK]
            fi = fs[(b - c) * rows:(b - c + 1) * rows, BLOCK:]
            hr = hs[c * rows:(c + 1) * rows, :BLOCK]
            hi = hs[c * rows:(c + 1) * rows, BLOCK:]
            re = re + (fr * hr - fi * hi)
            im = im + (fr * hi + fi * hr)
        ws[b * rows:(b + 1) * rows, :BLOCK] = re
        ws[b * rows:(b + 1) * rows, BLOCK:] = im
    wide = dot3(ws[...], b_table[...])
    for b in range(tblocks):
        y = wide[b * rows:(b + 1) * rows, :BLOCK]
        if b:
            y = y + wide[(b - 1) * rows:b * rows, BLOCK:]
        store(b, y.astype(BF16))


def when(cond, body):
    if cond is None:
        body()
    else:
        pl.when(cond)(body)


def both(a, b):
    if a is None:
        return b
    return a if b is None else a & b


LEVELS = 32000.0


def main_kernel(
    ny, tile, a_hbm, p_hbm, k_hbm, len_hbm, s_hbm, g_hbm, ft_hbm, bt_hbm,
    acc_ref, big, slast_ref,
    a_ref, p_ref, len_ref, g_ref, f_table, b_table, in_sem,
    k_own, shapes, forces, fcore, coded, codes, scaled, scales, steps, fall, mod, xs, xf, fs, hs, ws, hot,
    k_sem, shape_sem, slast_sem, core_send, core_recv, code_send, code_recv, scale_send, scale_recv, own_sem,
    m_send, recv, s_up0, s_down0, s_y0, s_up, s_down, s_y, s_relief,
):
    groups, ways, chunks, rows, slab = big.shape
    share = chunks * rows
    halves = recv.shape[2]
    part = chunks // halves
    dofs = acc_ref.shape[0]
    per_group = ways * share
    nz = groups // ny
    split = shapes.shape[0] == groups
    i, j = lax.axis_index("mode"), lax.axis_index("tm")
    z, y = i // ny, lax.rem(i, ny)
    below, above = z > 0, z < nz - 1
    relief = ny == 2 and nz >= 4 and ways >= 4
    mate = j + 1 - 2 * lax.rem(j, 2)

    def peer(d):
        return lax.rem(j // 2 + d // 2, ways // 2) * 2 + lax.rem(lax.rem(j, 2) + d, 2)

    loads = [
        pltpu.make_async_copy(src, dst, in_sem.at[n])
        for n, (src, dst) in enumerate((
            (a_hbm, a_ref), (p_hbm, p_ref), (len_hbm, len_ref), (ft_hbm, f_table), (bt_hbm, b_table), (g_hbm, g_ref),
        ))
    ]
    first = j * share
    k_copy = pltpu.make_async_copy(k_hbm.at[pl.ds(pl.multiple_of(first, share), share)], k_own, k_sem)
    loads[0].start()
    loads[1].start()

    barrier = pltpu.get_barrier_semaphore()

    def greet(mode, tm):
        pl.semaphore_signal(barrier, inc=1, device_id={"mode": mode, "tm": tm}, device_id_type=MESH)

    for d in range(1, ways):
        greet(i, lax.rem(j + d, ways))
    for tm in (j, mate):
        for e in range(1, ny):
            greet(z * ny + lax.rem(y + e, ny), tm)
        if nz > 1:
            @pl.when(below)
            def _():
                greet(i - ny, tm)

            @pl.when(above)
            def _():
                greet(i + ny, tm)

    lanes = scaled.shape[2]
    pair = 2 * share
    loads[0].wait()
    loads[1].wait()

    def forces_of(chip):
        rows = p_ref[pl.ds(pl.multiple_of(chip * pair, pair), pair), :]
        return jnp.dot(rows, a_ref[...], preferred_element_type=F32)

    for c in range(1, ways // 2):
        chip = lax.rem(j // 2 + c, ways // 2)
        values = forces_of(chip)
        top = jnp.max(jnp.abs(values), axis=1, keepdims=True)
        scale = (top * 1.01 + 1e-30).astype(BF16).astype(F32)
        values = jnp.round(values * (LEVELS / scale)).astype(jnp.int32).astype(jnp.int16)
        for core in range(2):
            at = core * share
            line = row_of(scale[at:at + share, :], lanes)
            scaled[chip * 2 + core] = jnp.broadcast_to(line, scaled.shape[1:]).astype(BF16)
            for h in range(chunks):
                coded[chip * 2 + core, h] = values[at + h * rows:at + (h + 1) * rows, :]

    always = ways - 1 + 2 * (ny - 1)
    if nz == 1:
        pl.semaphore_wait(barrier, always)
    else:
        @pl.when(below & above)
        def _():
            pl.semaphore_wait(barrier, always + 4)

        @pl.when(jnp.logical_not(below & above))
        def _():
            pl.semaphore_wait(barrier, always + 2)

    started = []

    def remote(src, dst, send_sem, recv_sem, mode, tm):
        return pltpu.make_async_remote_copy(
            src, dst, send_sem, recv_sem, device_id={"mode": mode, "tm": tm}, device_id_type=MESH,
        )

    def code_copy(d, h):
        return remote(coded.at[peer(d), h], codes.at[d, h], code_send.at[d, h], code_recv.at[d, h], i, peer(d))

    def scale_copy(d):
        return remote(scaled.at[peer(d)], scales.at[d], scale_send.at[d], scale_recv.at[d], i, peer(d))

    core_copy = remote(forces.at[pl.ds(pl.multiple_of(lax.rem(mate, 2) * share, share), share)], fcore, core_send, core_recv, i, mate)
    for d in range(2, ways):
        scale_copy(d).start()
        started.append(functools.partial(scale_copy, d))
    for h in range(chunks):
        for d in range(2, ways):
            code_copy(d, h).start()
            started.append(functools.partial(code_copy, d, h))

    for load in loads[2:]:
        load.start()
    k_copy.start()
    forces[...] = forces_of(j // 2)
    core_copy.start()
    started.append(lambda: core_copy)

    def columns(g):
        return s_hbm.at[:, pl.ds(pl.multiple_of(g * per_group, per_group), per_group)]

    glast = last_group(i, ny, nz)
    shape_copies = []
    if split:
        for d in range(groups):
            g = lax.rem(i + d, groups)
            shape_copies.append(pltpu.make_async_copy(columns(g), shapes.at[g], shape_sem.at[d]))
        shape_copies.append(pltpu.make_async_copy(columns(glast), slast_ref, slast_sem))
    else:
        shape_copies.append(pltpu.make_async_copy(s_hbm, shapes.at[0], shape_sem.at[0]))
    for copy in shape_copies:
        copy.start()

    for load in loads[2:]:
        load.wait()
    k_copy.wait()
    taps_spectrum(first, k_own, len_ref, xs, hs, f_table)

    per = slab // BLOCK
    back = [d if d < 2 else (ways // 2 - d // 2) * 2 + d % 2 for d in range(ways)]
    for d in range(2, ways):
        scale_copy(d).wait_recv()
    for d in range(2, ways):
        column = column_of(scales[back[d], 0:1, :].astype(F32), share) * (1 / LEVELS)
        for h in range(chunks):
            steps[d, h] = jnp.broadcast_to(column[h * rows:(h + 1) * rows, :], steps.shape[2:])
    core_copy.wait_recv()

    def hops(h):
        dst, sem = big.at[i, j, h], recv.at[i, j, h // part]
        made = []
        for d in range(2, ways):
            made.append((None, remote(mod.at[h, peer(d)], dst, m_send.at[d, h], sem, i, peer(d))))
        for n, tm in enumerate((j, mate)):
            src = mod.at[h, tm]
            for e in range(1, ny):
                made.append((None, remote(src, dst, s_y0.at[e - 1, n, h], sem, z * ny + lax.rem(y + e, ny), tm)))
            if nz > 1:
                made.append((above, remote(src, dst, s_up0.at[n, h], sem, i + ny, tm)))
                made.append((below, remote(src, dst, s_down0.at[n, h], sem, i - ny, tm)))
        made.append((None, remote(mod.at[h, mate], dst, m_send.at[1, h], sem, i, mate)))
        return made

    def chunk(h, carry):
        for d in range(2, ways):
            code_copy(d, h).wait_recv()
        at = pl.ds(pl.multiple_of(h * rows, rows), rows)
        fall[j] = forces[pl.ds(pl.multiple_of(lax.rem(j, 2) * share + h * rows, rows), rows), :]
        fall[mate] = fcore[at, :]
        for d in range(2, ways):
            fall[peer(d)] = codes[back[d], h].astype(jnp.int32).astype(F32) * steps[d, h, :, 0:1]
        blocks = [fall[b // per, :, (b % per) * BLOCK:(b % per + 1) * BLOCK] for b in range(ways * per)]

        def store(b, value):
            mod[h, b // per, :, (b % per) * BLOCK:(b % per + 1) * BLOCK] = value

        filter_rows(blocks, store, hs.at[h], xf, fs, ws, f_table, b_table)
        for cond, copy in hops(h):
            when(cond, copy.start)
        big[i, j, h] = mod[h, j]
        return carry

    lax.fori_loop(0, chunks, chunk, 0)

    pending = []

    def half(g, q, k):
        return big.at[g, q, pl.ds(k * part, part)]

    def send(cond, g, q, k, sem, mode, tm):
        def make():
            return remote(half(g, q, k), half(g, q, k), sem.at[k], recv.at[g, q, k], mode, tm)
        when(cond, lambda: make().start())
        pending.append((cond, make))

    def sent(n):
        for cond, make in pending[:n]:
            when(cond, lambda: make().wait_send())
        del pending[:n]

    def arrived(cond, g, q, k):
        when(cond, lambda: remote(half(g, q, k), half(g, q, k), own_sem, recv.at[g, q, k], i, j).wait_recv())

    lane = g_ref.shape[1]
    work = collections.deque()

    def ground(r):
        for part in range(tile // lane):
            at = r * (tile // lane) + part
            column = column_of(g_ref[at:at + 1, :].astype(F32), lane)
            support = lax.broadcasted_iota(jnp.int32, (lane, a_ref.shape[0]), 1).astype(F32)
            hot[part * lane:(part + 1) * lane, :] = (support == column).astype(F32).astype(BF16)
        acc_ref[r * tile:(r + 1) * tile, :] = jnp.dot(hot[...], a_ref[...], preferred_element_type=F32)

    for r in range(dofs // tile):
        work.append((None, functools.partial(ground, r)))

    def product(cond, g):
        if not split:
            return

        def unit(r):
            at = pl.ds(r * tile, tile)
            block = big[g].reshape(per_group, slab)
            acc_ref[at, :] += jnp.dot(shapes[g, at, :], block, preferred_element_type=F32)
        for r in range(dofs // tile):
            work.append((cond, functools.partial(unit, r)))

    def drain(n):
        for _ in range(min(n, len(work))):
            cond, unit = work.popleft()
            when(cond, unit)

    def across(cond, g, q, k, slot, d):
        for e in range(1, ny):
            send(cond, g, q, k, s_y.at[slot, e - 1, d], z * ny + lax.rem(y + e, ny), j)

    def up(cond, g, q, k, slot, d):
        if nz > 1:
            send(both(cond, above), g, q, k, s_up.at[slot, d], i + ny, j)

    def down(cond, g, q, k, slot, d):
        if nz > 1:
            send(both(cond, below), g, q, k, s_down.at[slot, d], i - ny, j)

    def own_event(d, k):
        q = peer(d)
        arrived(None, i, q, k)
        if d >= 2:
            across(None, i, q, k, 0, d)
            down(None, i, q, k, 0, d)
            up(None, i, q, k, 0, d)

    def column_event(s, d, k):
        q = peer(d)
        lower, upper = i - s * ny, i + s * ny
        has_low, has_high = z - s >= 0, z + s <= nz - 1
        far = relief and s == nz - 1 and 2 * d >= ways
        near = relief and s == 1
        arrived(has_high, upper, q, k)
        if not far:
            across(both(has_high, z != nz - 2 if near else None), upper, q, k, nz - 1 + s, d)
        down(has_high, upper, q, k, s, d)
        arrived(has_low, lower, q, k)
        if not far:
            across(both(has_low, z != 1 if near else None), lower, q, k, s, d)
        up(has_low, lower, q, k, s, d)

    def other_event(s, d, k):
        q = peer(d)
        for e in range(1, ny):
            line = lax.rem(y + e, ny)
            if s == 0:
                g = z * ny + line
                arrived(None, g, q, k)
                if relief:
                    send(z == 0, g, q, k, s_relief.at[0, d], i + ny, j)
                    send(z == nz - 1, g, q, k, s_relief.at[0, d], i - ny, j)
                continue
            lower, upper = (z - s) * ny + line, (z + s) * ny + line
            arrived(z - s >= 0, lower, q, k)
            arrived(z + s <= nz - 1, upper, q, k)
            if relief and s == nz - 2 and 2 * d >= ways:
                send(z == nz - 2, lower, q, k, s_relief.at[1, d], i + ny, j)
                send(z == 1, upper, q, k, s_relief.at[1, d], i - ny, j)

    def other_products(s):
        for e in range(1, ny):
            line = lax.rem(y + e, ny)
            if s == 0:
                g = z * ny + line
                product(g != glast, g)
                continue
            for level, there in ((z - s, z - s >= 0), (z + s, z + s <= nz - 1)):
                g = level * ny + line
                product(there & (g != glast), g)

    for copy in shape_copies:
        copy.wait()
    near_ones, far_ones = range(min(2, ways)), range(2, ways)
    for k in range(halves):
        for d in near_ones:
            if nz > 1:
                column_event(1, d, k)
            for f in far_ones:
                if f % 2 == d:
                    own_event(f, k)
        own_event(1, k)
        for d in near_ones:
            other_event(0, d, k)
        drain(1)
    product(None, i)
    for k in range(halves):
        for d in far_ones:
            if nz > 1:
                column_event(1, d, k)
            other_event(0, d, k)
            drain(1)
    before = len(pending)
    for s in range(2, nz):
        product(z - s + 1 >= 0, i - (s - 1) * ny)
        product(z + s - 1 <= nz - 1, i + (s - 1) * ny)
        other_products(s - 2)
        if s == 2:
            for make in started:
                make().wait_send()

            def hopped(h, carry):
                for cond, copy in hops(h):
                    when(cond, copy.wait_send)
                return carry

            lax.fori_loop(0, chunks, hopped, 0)
        else:
            sent(before)
            before = len(pending)
        for some in (near_ones, far_ones):
            for k in range(halves):
                for d in some:
                    column_event(s, d, k)
                    other_event(s - 1, d, k)
                    drain(1)
    if nz > 1:
        s = nz - 1
        product(z - s >= 0, i - s * ny)
        product(z + s <= nz - 1, i + s * ny)
    other_products(max(nz - 2, 0))
    drain(len(work))
    if nz <= 2:
        for make in started:
            make().wait_send()
        for h in range(chunks):
            for cond, copy in hops(h):
                when(cond, copy.wait_send)
    sent(before)
    if nz > 1:
        for d in range(ways):
            for k in range(halves):
                other_event(nz - 1, d, k)
        other_products(nz - 1)
    drain(len(work))
    if not split:
        def whole(r, carry):
            at = pl.ds(pl.multiple_of(r * tile, tile), tile)
            block = big[...].reshape(groups * per_group, slab)
            acc_ref[at, :] += jnp.dot(shapes[0, at, :], block, preferred_element_type=F32)
            return carry
        lax.fori_loop(0, dofs // tile, whole, 0)
    sent(len(pending))


def tail_kernel(ny, tile, acc_ref, big, s_ref, o_hbm, out, sem):
    groups, ways, chunks, rows, slab = big.shape
    glast = last_group(lax.axis_index("mode"), ny, groups // ny)
    dofs = acc_ref.shape[0]
    copies = []
    for n in range(dofs // tile):
        at = pl.ds(n * tile, tile)
        total = acc_ref[at, :]
        if s_ref.shape[0] == dofs:
            block = big[glast].reshape(ways * chunks * rows, slab)
            total += jnp.dot(s_ref[at, :], block, preferred_element_type=F32)
        out[at, :] = total.astype(BF16)
        copies.append(pltpu.make_async_copy(out.at[at], o_hbm.at[at], sem.at[n]))
        copies[-1].start()
    for copy in copies:
        copy.wait()


def per_device(support_accel, participation, kernels, lengths, mode_shapes, groups):
    ways, ngroups = lax.axis_size("tm"), lax.axis_size("mode")
    ny, nz = grid_of(ngroups, ways)
    held, taps = kernels.shape
    share = held // ways
    rows = 16 if share % 16 == 0 else share
    chunks = share // rows
    halves = 2 if chunks % 2 == 0 else 1
    supports, slab = support_accel.shape
    dofs, modes = mode_shapes.shape
    tile = min(1024, dofs)
    last_tile = min(256, dofs)
    split = held % 128 == 0 and ny > 1 and dofs > tile
    times = ways * slab
    lanes = -(-share // 128) * 128
    tables = transform_tables()
    hbm = pl.BlockSpec(memory_space=pltpu.HBM)
    vmem = pl.BlockSpec(memory_space=pltpu.VMEM)
    dma = pltpu.SemaphoreType.DMA
    acc, every, shapes = pl.pallas_call(
        functools.partial(main_kernel, ny, tile),
        out_shape=(
            pltpu.VMEM((dofs, slab), F32),
            pltpu.VMEM((ngroups, ways, chunks, rows, slab), BF16),
            pltpu.VMEM((dofs, held) if split else (16, 128), BF16),
        ),
        in_specs=[hbm] * 8,
        out_specs=(vmem, vmem, vmem),
        scratch_shapes=[
            pltpu.VMEM((supports, slab), BF16),
            pltpu.VMEM((held, supports), BF16),
            pltpu.VMEM((1, held), jnp.int32),
            pltpu.VMEM((dofs // 128, 128), jnp.int32),
            *(pltpu.VMEM(table.shape, BF16) for table in tables),
            dma((6,)),
            pltpu.VMEM((share, taps), F32),
            pltpu.VMEM((ngroups, dofs, held) if split else (1, dofs, modes), BF16),
            pltpu.VMEM((2 * share, slab), F32),
            pltpu.VMEM((share, slab), F32),
            pltpu.VMEM((ways, chunks, rows, slab), jnp.int16),
            pltpu.VMEM((ways, chunks, rows, slab), jnp.int16),
            pltpu.VMEM((ways, 16, lanes), BF16),
            pltpu.VMEM((ways, 16, lanes), BF16),
            pltpu.VMEM((ways, chunks, rows, 128), F32),
            pltpu.VMEM((ways, rows, slab), F32),
            pltpu.VMEM((chunks, ways, rows, slab), BF16),
            pltpu.VMEM((chunks, taps // BLOCK * rows, BLOCK), F32),
            pltpu.VMEM((times // BLOCK * rows, BLOCK), F32),
            pltpu.VMEM((times // BLOCK * rows, 2 * BLOCK), F32),
            pltpu.VMEM((chunks, taps // BLOCK * rows, 2 * BLOCK), F32),
            pltpu.VMEM((times // BLOCK * rows, 2 * BLOCK), F32),
            pltpu.VMEM((tile, supports), BF16),
            dma, dma((ngroups,)), dma, dma, dma, dma((ways, chunks)), dma((ways, chunks)), dma((ways,)), dma((ways,)), dma,
            dma((ways, chunks)), dma((ngroups, ways, halves)),
            dma((2, chunks)), dma((2, chunks)), dma((max(ny - 1, 1), 2, chunks)),
            dma((nz, ways, halves)), dma((nz, ways, halves)), dma((2 * nz - 1, max(ny - 1, 1), ways, halves)),
            dma((2, ways, halves)),
        ],
        compiler_params=pltpu.CompilerParams(
            collective_id=0, has_side_effects=True, vmem_limit_bytes=40 << 20
        ),
    )(*(pltpu.with_memory_space_constraint(array, pltpu.HBM) for array in (
        support_accel, participation, kernels, lengths.reshape(1, held), mode_shapes,
        groups.reshape(dofs // 128, 128), *map(jnp.asarray, tables),
    )))
    return pl.pallas_call(
        functools.partial(tail_kernel, ny, last_tile),
        out_shape=jax.ShapeDtypeStruct((dofs, slab), BF16),
        in_specs=[vmem, vmem, vmem],
        out_specs=hbm,
        scratch_shapes=[pltpu.VMEM((dofs, slab), BF16), dma((dofs // last_tile,))],
        compiler_params=pltpu.CompilerParams(vmem_limit_bytes=24 << 20),
    )(acc, every, shapes)


def solution(mesh):
    placed = (
        P(None, "tm"),
        P("mode", None),
        P("mode", None),
        P("mode"),
        P("mode", None),
        P("mode"),
    )
    return jax.shard_map(
        per_device, mesh=mesh, in_specs=placed, out_specs=P("mode", "tm"), check_vma=False
    )
```

```python
import collections
import functools

import jax
import jax.numpy as jnp
import numpy as np
from jax import lax
from jax.experimental import pallas as pl
from jax.experimental.pallas import tpu as pltpu
from jax.sharding import PartitionSpec as P

BLOCK = 128
F32 = jnp.float32
BF16 = jnp.bfloat16
MESH = pl.DeviceIdType.MESH


def split_constant(table):
    high = table.astype(BF16)
    low = (table - high.astype(np.float64)).astype(BF16)
    return high, low


def transform_tables():
    angle = np.pi * (np.arange(BLOCK)[:, None] + 0.5) / BLOCK
    time = np.arange(2 * BLOCK)[None, :]
    cos, sin = np.cos(angle * time), np.sin(angle * time)
    forward = np.concatenate([cos[:, :BLOCK], -sin[:, :BLOCK]], axis=0).T
    backward = np.concatenate([cos, -sin], axis=0) / BLOCK
    tables = []
    for table in (forward, backward):
        high, low = split_constant(table)
        tables.append(np.concatenate([high, high, low], axis=0))
    return tables


def dot3(values, table):
    top = values.astype(BF16)
    rest = (values - top.astype(F32)).astype(BF16)
    return jnp.dot(jnp.concatenate([top, rest, top], axis=1), table, preferred_element_type=F32)


def grid_of(groups, ways):
    ny = max(ways // 2, 1)
    if groups % ny:
        ny = 1
    return ny, groups // ny


def last_group(i, ny, nz):
    z, y = i // ny, lax.rem(i, ny)
    far = jnp.where(2 * z < nz, nz - 1, 0)
    return far * ny + lax.rem(y + 1, ny)


def column_of(row, rows):
    lanes = row.shape[1]
    at = lax.broadcasted_iota(jnp.int32, (rows, lanes), 0) == lax.broadcasted_iota(jnp.int32, (rows, lanes), 1)
    return jnp.sum(jnp.where(at, jnp.broadcast_to(row, (rows, lanes)), 0.0), axis=1, keepdims=True)


def row_of(column, lanes):
    rows = column.shape[0]
    at = lax.broadcasted_iota(jnp.int32, (rows, lanes), 0) == lax.broadcasted_iota(jnp.int32, (rows, lanes), 1)
    return jnp.sum(jnp.where(at, jnp.broadcast_to(column, (rows, lanes)), 0.0), axis=0, keepdims=True)


def taps_spectrum(first, k_own, len_ref, xs, hs, f_table):
    share, taps = k_own.shape
    chunks = hs.shape[0]
    rows = share // chunks
    held = len_ref.shape[1]
    picked = lax.broadcasted_iota(jnp.int32, (share, held), 1) == first + lax.broadcasted_iota(jnp.int32, (share, held), 0)
    wide = jnp.broadcast_to(len_ref[...], (share, held)).astype(F32)
    lengths = jnp.sum(jnp.where(picked, wide, 0.0), axis=1, keepdims=True)
    kblocks = taps // BLOCK
    for c in range(kblocks):
        pos = (c * BLOCK + lax.broadcasted_iota(jnp.int32, (share, BLOCK), 1)).astype(F32)
        part = k_own[:, c * BLOCK:(c + 1) * BLOCK]
        part = jnp.where(pos < lengths, part, jnp.zeros_like(part))
        for h in range(chunks):
            xs[h, c * rows:(c + 1) * rows, :] = part[h * rows:(h + 1) * rows, :]
    for h in range(chunks):
        hs[h] = dot3(xs[h, :kblocks * rows, :], f_table[...])


def filter_rows(blocks, store, hs, xs, fs, ws, f_table, b_table):
    tblocks = len(blocks)
    rows = blocks[0].shape[0]
    kblocks = hs.shape[0] // rows
    for a in range(tblocks):
        xs[a * rows:(a + 1) * rows, :] = blocks[a]
    fs[...] = dot3(xs[:tblocks * rows, :], f_table[...])
    for b in range(tblocks):
        re = jnp.zeros((rows, BLOCK), F32)
        im = jnp.zeros((rows, BLOCK), F32)
        for c in range(min(b + 1, kblocks)):
            fr = fs[(b - c) * rows:(b - c + 1) * rows, :BLOCK]
            fi = fs[(b - c) * rows:(b - c + 1) * rows, BLOCK:]
            hr = hs[c * rows:(c + 1) * rows, :BLOCK]
            hi = hs[c * rows:(c + 1) * rows, BLOCK:]
            re = re + (fr * hr - fi * hi)
            im = im + (fr * hi + fi * hr)
        ws[b * rows:(b + 1) * rows, :BLOCK] = re
        ws[b * rows:(b + 1) * rows, BLOCK:] = im
    wide = dot3(ws[...], b_table[...])
    for b in range(tblocks):
        y = wide[b * rows:(b + 1) * rows, :BLOCK]
        if b:
            y = y + wide[(b - 1) * rows:b * rows, BLOCK:]
        store(b, y.astype(BF16))


def when(cond, body):
    if cond is None:
        body()
    else:
        pl.when(cond)(body)


def both(a, b):
    if a is None:
        return b
    return a if b is None else a & b


LEVELS = 32000.0


def main_kernel(
    ny, tile, a_hbm, p_hbm, k_hbm, len_hbm, s_hbm, g_hbm, ft_hbm, bt_hbm,
    acc_ref, big, slast_ref,
    a_ref, p_ref, len_ref, g_ref, f_table, b_table, in_sem,
    k_own, shapes, forces, fcore, coded, codes, scaled, scales, steps, fall, mod, xs, xf, fs, hs, ws, hot,
    k_sem, shape_sem, slast_sem, core_send, core_recv, code_send, code_recv, scale_send, scale_recv, own_sem,
    m_send, recv, s_up0, s_down0, s_y0, s_up, s_down, s_y, s_relief,
):
    groups, ways, chunks, rows, slab = big.shape
    share = chunks * rows
    halves = recv.shape[2]
    part = chunks // halves
    dofs = acc_ref.shape[0]
    per_group = ways * share
    nz = groups // ny
    split = shapes.shape[0] == groups
    i, j = lax.axis_index("mode"), lax.axis_index("tm")
    z, y = i // ny, lax.rem(i, ny)
    below, above = z > 0, z < nz - 1
    relief = ny == 2 and nz >= 4 and ways >= 4
    mate = j + 1 - 2 * lax.rem(j, 2)

    def peer(d):
        return lax.rem(j // 2 + d // 2, ways // 2) * 2 + lax.rem(lax.rem(j, 2) + d, 2)

    loads = [
        pltpu.make_async_copy(src, dst, in_sem.at[n])
        for n, (src, dst) in enumerate((
            (a_hbm, a_ref), (p_hbm, p_ref), (len_hbm, len_ref), (ft_hbm, f_table), (bt_hbm, b_table), (g_hbm, g_ref),
        ))
    ]
    first = j * share
    k_copy = pltpu.make_async_copy(k_hbm.at[pl.ds(pl.multiple_of(first, share), share)], k_own, k_sem)
    loads[0].start()
    loads[1].start()

    barrier = pltpu.get_barrier_semaphore()

    def greet(mode, tm):
        pl.semaphore_signal(barrier, inc=1, device_id={"mode": mode, "tm": tm}, device_id_type=MESH)

    for d in range(1, ways):
        greet(i, lax.rem(j + d, ways))
    for tm in (j, mate):
        for e in range(1, ny):
            greet(z * ny + lax.rem(y + e, ny), tm)
        if nz > 1:
            @pl.when(below)
            def _():
                greet(i - ny, tm)

            @pl.when(above)
            def _():
                greet(i + ny, tm)

    lanes = scaled.shape[2]
    pair = 2 * share
    loads[0].wait()
    loads[1].wait()

    def forces_of(chip):
        rows = p_ref[pl.ds(pl.multiple_of(chip * pair, pair), pair), :]
        return jnp.dot(rows, a_ref[...], preferred_element_type=F32)

    for c in range(1, ways // 2):
        chip = lax.rem(j // 2 + c, ways // 2)
        values = forces_of(chip)
        top = jnp.max(jnp.abs(values), axis=1, keepdims=True)
        scale = (top * 1.01 + 1e-30).astype(BF16).astype(F32)
        values = jnp.round(values * (LEVELS / scale)).astype(jnp.int32).astype(jnp.int16)
        for core in range(2):
            at = core * share
            line = row_of(scale[at:at + share, :], lanes)
            scaled[chip * 2 + core] = jnp.broadcast_to(line, scaled.shape[1:]).astype(BF16)
            for h in range(chunks):
                coded[chip * 2 + core, h] = values[at + h * rows:at + (h + 1) * rows, :]

    always = ways - 1 + 2 * (ny - 1)
    if nz == 1:
        pl.semaphore_wait(barrier, always)
    else:
        @pl.when(below & above)
        def _():
            pl.semaphore_wait(barrier, always + 4)

        @pl.when(jnp.logical_not(below & above))
        def _():
            pl.semaphore_wait(barrier, always + 2)

    started = []

    def remote(src, dst, send_sem, recv_sem, mode, tm):
        return pltpu.make_async_remote_copy(
            src, dst, send_sem, recv_sem, device_id={"mode": mode, "tm": tm}, device_id_type=MESH,
        )

    def code_copy(d, h):
        return remote(coded.at[peer(d), h], codes.at[d, h], code_send.at[d, h], code_recv.at[d, h], i, peer(d))

    def scale_copy(d):
        return remote(scaled.at[peer(d)], scales.at[d], scale_send.at[d], scale_recv.at[d], i, peer(d))

    core_copy = remote(forces.at[pl.ds(pl.multiple_of(lax.rem(mate, 2) * share, share), share)], fcore, core_send, core_recv, i, mate)
    for d in range(2, ways):
        scale_copy(d).start()
        started.append(functools.partial(scale_copy, d))
    for h in range(chunks):
        for d in range(2, ways):
            code_copy(d, h).start()
            started.append(functools.partial(code_copy, d, h))

    for load in loads[2:]:
        load.start()
    k_copy.start()
    forces[...] = forces_of(j // 2)
    core_copy.start()
    started.append(lambda: core_copy)

    def columns(g):
        return s_hbm.at[:, pl.ds(pl.multiple_of(g * per_group, per_group), per_group)]

    glast = last_group(i, ny, nz)
    shape_copies = []
    if split:
        for d in range(groups):
            g = lax.rem(i + d, groups)
            shape_copies.append(pltpu.make_async_copy(columns(g), shapes.at[g], shape_sem.at[d]))
        shape_copies.append(pltpu.make_async_copy(columns(glast), slast_ref, slast_sem))
    else:
        shape_copies.append(pltpu.make_async_copy(s_hbm, shapes.at[0], shape_sem.at[0]))
    for copy in shape_copies:
        copy.start()

    for load in loads[2:]:
        load.wait()
    k_copy.wait()
    taps_spectrum(first, k_own, len_ref, xs, hs, f_table)

    per = slab // BLOCK
    back = [d if d < 2 else (ways // 2 - d // 2) * 2 + d % 2 for d in range(ways)]
    for d in range(2, ways):
        scale_copy(d).wait_recv()
    for d in range(2, ways):
        column = column_of(scales[back[d], 0:1, :].astype(F32), share) * (1 / LEVELS)
        for h in range(chunks):
            steps[d, h] = jnp.broadcast_to(column[h * rows:(h + 1) * rows, :], steps.shape[2:])
    core_copy.wait_recv()

    def hops(h):
        dst, sem = big.at[i, j, h], recv.at[i, j, h // part]
        made = []
        for d in range(2, ways):
            made.append((None, remote(mod.at[h, peer(d)], dst, m_send.at[d, h], sem, i, peer(d))))
        for n, tm in enumerate((j, mate)):
            src = mod.at[h, tm]
            for e in range(1, ny):
                made.append((None, remote(src, dst, s_y0.at[e - 1, n, h], sem, z * ny + lax.rem(y + e, ny), tm)))
            if nz > 1:
                made.append((above, remote(src, dst, s_up0.at[n, h], sem, i + ny, tm)))
                made.append((below, remote(src, dst, s_down0.at[n, h], sem, i - ny, tm)))
        made.append((None, remote(mod.at[h, mate], dst, m_send.at[1, h], sem, i, mate)))
        return made

    def chunk(h, carry):
        for d in range(2, ways):
            code_copy(d, h).wait_recv()
        at = pl.ds(pl.multiple_of(h * rows, rows), rows)
        fall[j] = forces[pl.ds(pl.multiple_of(lax.rem(j, 2) * share + h * rows, rows), rows), :]
        fall[mate] = fcore[at, :]
        for d in range(2, ways):
            fall[peer(d)] = codes[back[d], h].astype(jnp.int32).astype(F32) * steps[d, h, :, 0:1]
        blocks = [fall[b // per, :, (b % per) * BLOCK:(b % per + 1) * BLOCK] for b in range(ways * per)]

        def store(b, value):
            mod[h, b // per, :, (b % per) * BLOCK:(b % per + 1) * BLOCK] = value

        filter_rows(blocks, store, hs.at[h], xf, fs, ws, f_table, b_table)
        for cond, copy in hops(h):
            when(cond, copy.start)
        big[i, j, h] = mod[h, j]
        return carry

    lax.fori_loop(0, chunks, chunk, 0)

    pending = []

    def half(g, q, k):
        return big.at[g, q, pl.ds(k * part, part)]

    def send(cond, g, q, k, sem, mode, tm):
        def make():
            return remote(half(g, q, k), half(g, q, k), sem.at[k], recv.at[g, q, k], mode, tm)
        when(cond, lambda: make().start())
        pending.append((cond, make))

    def sent(n):
        for cond, make in pending[:n]:
            when(cond, lambda: make().wait_send())
        del pending[:n]

    def arrived(cond, g, q, k):
        when(cond, lambda: remote(half(g, q, k), half(g, q, k), own_sem, recv.at[g, q, k], i, j).wait_recv())

    lane = g_ref.shape[1]
    work = collections.deque()

    def ground(r):
        for part in range(tile // lane):
            at = r * (tile // lane) + part
            column = column_of(g_ref[at:at + 1, :].astype(F32), lane)
            support = lax.broadcasted_iota(jnp.int32, (lane, a_ref.shape[0]), 1).astype(F32)
            hot[part * lane:(part + 1) * lane, :] = (support == column).astype(F32).astype(BF16)
        acc_ref[r * tile:(r + 1) * tile, :] = jnp.dot(hot[...], a_ref[...], preferred_element_type=F32)

    for r in range(dofs // tile):
        work.append((None, functools.partial(ground, r)))

    def product(cond, g):
        if not split:
            return

        def unit(r):
            at = pl.ds(r * tile, tile)
            block = big[g].reshape(per_group, slab)
            acc_ref[at, :] += jnp.dot(shapes[g, at, :], block, preferred_element_type=F32)
        for r in range(dofs // tile):
            work.append((cond, functools.partial(unit, r)))

    def drain(n):
        for _ in range(min(n, len(work))):
            cond, unit = work.popleft()
            when(cond, unit)

    def across(cond, g, q, k, slot, d):
        for e in range(1, ny):
            send(cond, g, q, k, s_y.at[slot, e - 1, d], z * ny + lax.rem(y + e, ny), j)

    def up(cond, g, q, k, slot, d):
        if nz > 1:
            send(both(cond, above), g, q, k, s_up.at[slot, d], i + ny, j)

    def down(cond, g, q, k, slot, d):
        if nz > 1:
            send(both(cond, below), g, q, k, s_down.at[slot, d], i - ny, j)

    def own_event(d, k):
        q = peer(d)
        arrived(None, i, q, k)
        if d >= 2:
            across(None, i, q, k, 0, d)
            down(None, i, q, k, 0, d)
            up(None, i, q, k, 0, d)

    def column_event(s, d, k):
        q = peer(d)
        lower, upper = i - s * ny, i + s * ny
        has_low, has_high = z - s >= 0, z + s <= nz - 1
        far = relief and s == nz - 1 and 2 * (d * halves + k) >= ways * halves + 2 * (ways * halves // 8)
        near = relief and s == 1
        arrived(has_high, upper, q, k)
        if not far:
            across(both(has_high, z != nz - 2 if near else None), upper, q, k, nz - 1 + s, d)
        down(has_high, upper, q, k, s, d)
        arrived(has_low, lower, q, k)
        if not far:
            across(both(has_low, z != 1 if near else None), lower, q, k, s, d)
        up(has_low, lower, q, k, s, d)

    def other_event(s, d, k):
        q = peer(d)
        for e in range(1, ny):
            line = lax.rem(y + e, ny)
            if s == 0:
                g = z * ny + line
                arrived(None, g, q, k)
                if relief:
                    send(z == 0, g, q, k, s_relief.at[0, d], i + ny, j)
                    send(z == nz - 1, g, q, k, s_relief.at[0, d], i - ny, j)
                continue
            lower, upper = (z - s) * ny + line, (z + s) * ny + line
            arrived(z - s >= 0, lower, q, k)
            arrived(z + s <= nz - 1, upper, q, k)
            if relief and s == nz - 2 and 2 * (d * halves + k) >= ways * halves + 2 * (ways * halves // 8):
                send(z == nz - 2, lower, q, k, s_relief.at[1, d], i + ny, j)
                send(z == 1, upper, q, k, s_relief.at[1, d], i - ny, j)

    def other_products(s):
        for e in range(1, ny):
            line = lax.rem(y + e, ny)
            if s == 0:
                g = z * ny + line
                product(g != glast, g)
                continue
            for level, there in ((z - s, z - s >= 0), (z + s, z + s <= nz - 1)):
                g = level * ny + line
                product(there & (g != glast), g)

    for copy in shape_copies:
        copy.wait()
    near_ones, far_ones = range(min(2, ways)), range(2, ways)
    for k in range(halves):
        for d in near_ones:
            if nz > 1:
                column_event(1, d, k)
            for f in far_ones:
                if f % 2 == d:
                    own_event(f, k)
        own_event(1, k)
        for d in near_ones:
            other_event(0, d, k)
        drain(1)
    product(None, i)
    for k in range(halves):
        for d in far_ones:
            if nz > 1:
                column_event(1, d, k)
            other_event(0, d, k)
            drain(1)
    before = len(pending)
    for s in range(2, nz):
        product(z - s + 1 >= 0, i - (s - 1) * ny)
        product(z + s - 1 <= nz - 1, i + (s - 1) * ny)
        other_products(s - 2)
        if s == 2:
            for make in started:
                make().wait_send()

            def hopped(h, carry):
                for cond, copy in hops(h):
                    when(cond, copy.wait_send)
                return carry

            lax.fori_loop(0, chunks, hopped, 0)
        else:
            sent(before)
            before = len(pending)
        for some in (near_ones, far_ones):
            for k in range(halves):
                for d in some:
                    column_event(s, d, k)
                    other_event(s - 1, d, k)
                    drain(1)
    if nz > 1:
        s = nz - 1
        product(z - s >= 0, i - s * ny)
        product(z + s <= nz - 1, i + s * ny)
    other_products(max(nz - 2, 0))
    drain(len(work))
    if nz <= 2:
        for make in started:
            make().wait_send()
        for h in range(chunks):
            for cond, copy in hops(h):
                when(cond, copy.wait_send)
    sent(before)
    if nz > 1:
        for d in range(ways):
            for k in range(halves):
                other_event(nz - 1, d, k)
        other_products(nz - 1)
    drain(len(work))
    if not split:
        def whole(r, carry):
            at = pl.ds(pl.multiple_of(r * tile, tile), tile)
            block = big[...].reshape(groups * per_group, slab)
            acc_ref[at, :] += jnp.dot(shapes[0, at, :], block, preferred_element_type=F32)
            return carry
        lax.fori_loop(0, dofs // tile, whole, 0)
    sent(len(pending))


def tail_kernel(ny, tile, acc_ref, big, s_ref, o_hbm, out, sem):
    groups, ways, chunks, rows, slab = big.shape
    glast = last_group(lax.axis_index("mode"), ny, groups // ny)
    dofs = acc_ref.shape[0]
    copies = []
    for n in range(dofs // tile):
        at = pl.ds(n * tile, tile)
        total = acc_ref[at, :]
        if s_ref.shape[0] == dofs:
            block = big[glast].reshape(ways * chunks * rows, slab)
            total += jnp.dot(s_ref[at, :], block, preferred_element_type=F32)
        out[at, :] = total.astype(BF16)
        copies.append(pltpu.make_async_copy(out.at[at], o_hbm.at[at], sem.at[n]))
        copies[-1].start()
    for copy in copies:
        copy.wait()


def per_device(support_accel, participation, kernels, lengths, mode_shapes, groups):
    ways, ngroups = lax.axis_size("tm"), lax.axis_size("mode")
    ny, nz = grid_of(ngroups, ways)
    held, taps = kernels.shape
    share = held // ways
    rows = 16 if share % 16 == 0 else share
    chunks = share // rows
    halves = 2 if chunks % 2 == 0 else 1
    supports, slab = support_accel.shape
    dofs, modes = mode_shapes.shape
    tile = min(1024, dofs)
    last_tile = min(256, dofs)
    split = held % 128 == 0 and ny > 1 and dofs > tile
    times = ways * slab
    lanes = -(-share // 128) * 128
    tables = transform_tables()
    hbm = pl.BlockSpec(memory_space=pltpu.HBM)
    vmem = pl.BlockSpec(memory_space=pltpu.VMEM)
    dma = pltpu.SemaphoreType.DMA
    acc, every, shapes = pl.pallas_call(
        functools.partial(main_kernel, ny, tile),
        out_shape=(
            pltpu.VMEM((dofs, slab), F32),
            pltpu.VMEM((ngroups, ways, chunks, rows, slab), BF16),
            pltpu.VMEM((dofs, held) if split else (16, 128), BF16),
        ),
        in_specs=[hbm] * 8,
        out_specs=(vmem, vmem, vmem),
        scratch_shapes=[
            pltpu.VMEM((supports, slab), BF16),
            pltpu.VMEM((held, supports), BF16),
            pltpu.VMEM((1, held), jnp.int32),
            pltpu.VMEM((dofs // 128, 128), jnp.int32),
            *(pltpu.VMEM(table.shape, BF16) for table in tables),
            dma((6,)),
            pltpu.VMEM((share, taps), F32),
            pltpu.VMEM((ngroups, dofs, held) if split else (1, dofs, modes), BF16),
            pltpu.VMEM((2 * share, slab), F32),
            pltpu.VMEM((share, slab), F32),
            pltpu.VMEM((ways, chunks, rows, slab), jnp.int16),
            pltpu.VMEM((ways, chunks, rows, slab), jnp.int16),
            pltpu.VMEM((ways, 16, lanes), BF16),
            pltpu.VMEM((ways, 16, lanes), BF16),
            pltpu.VMEM((ways, chunks, rows, 128), F32),
            pltpu.VMEM((ways, rows, slab), F32),
            pltpu.VMEM((chunks, ways, rows, slab), BF16),
            pltpu.VMEM((chunks, taps // BLOCK * rows, BLOCK), F32),
            pltpu.VMEM((times // BLOCK * rows, BLOCK), F32),
            pltpu.VMEM((times // BLOCK * rows, 2 * BLOCK), F32),
            pltpu.VMEM((chunks, taps // BLOCK * rows, 2 * BLOCK), F32),
            pltpu.VMEM((times // BLOCK * rows, 2 * BLOCK), F32),
            pltpu.VMEM((tile, supports), BF16),
            dma, dma((ngroups,)), dma, dma, dma, dma((ways, chunks)), dma((ways, chunks)), dma((ways,)), dma((ways,)), dma,
            dma((ways, chunks)), dma((ngroups, ways, halves)),
            dma((2, chunks)), dma((2, chunks)), dma((max(ny - 1, 1), 2, chunks)),
            dma((nz, ways, halves)), dma((nz, ways, halves)), dma((2 * nz - 1, max(ny - 1, 1), ways, halves)),
            dma((2, ways, halves)),
        ],
        compiler_params=pltpu.CompilerParams(
            collective_id=0, has_side_effects=True, vmem_limit_bytes=40 << 20
        ),
    )(*(pltpu.with_memory_space_constraint(array, pltpu.HBM) for array in (
        support_accel, participation, kernels, lengths.reshape(1, held), mode_shapes,
        groups.reshape(dofs // 128, 128), *map(jnp.asarray, tables),
    )))
    return pl.pallas_call(
        functools.partial(tail_kernel, ny, last_tile),
        out_shape=jax.ShapeDtypeStruct((dofs, slab), BF16),
        in_specs=[vmem, vmem, vmem],
        out_specs=hbm,
        scratch_shapes=[pltpu.VMEM((dofs, slab), BF16), dma((dofs // last_tile,))],
        compiler_params=pltpu.CompilerParams(vmem_limit_bytes=24 << 20),
    )(acc, every, shapes)


def solution(mesh):
    placed = (
        P(None, "tm"),
        P("mode", None),
        P("mode", None),
        P("mode"),
        P("mode", None),
        P("mode"),
    )
    return jax.shard_map(
        per_device, mesh=mesh, in_specs=placed, out_specs=P("mode", "tm"), check_vma=False
    )
```

```python
import collections
import functools

import jax
import jax.numpy as jnp
import numpy as np
from jax import lax
from jax.experimental import pallas as pl
from jax.experimental.pallas import tpu as pltpu
from jax.sharding import PartitionSpec as P

BLOCK = 128
F32 = jnp.float32
BF16 = jnp.bfloat16
MESH = pl.DeviceIdType.MESH


def split_constant(table):
    high = table.astype(BF16)
    low = (table - high.astype(np.float64)).astype(BF16)
    return high, low


def transform_tables():
    angle = np.pi * (np.arange(BLOCK)[:, None] + 0.5) / BLOCK
    time = np.arange(2 * BLOCK)[None, :]
    cos, sin = np.cos(angle * time), np.sin(angle * time)
    forward = np.concatenate([cos[:, :BLOCK], -sin[:, :BLOCK]], axis=0).T
    backward = np.concatenate([cos, -sin], axis=0) / BLOCK
    tables = []
    for table in (forward, backward):
        high, low = split_constant(table)
        tables.append(np.concatenate([high, high, low], axis=0))
    return tables


def dot3(values, table):
    top = values.astype(BF16)
    rest = (values - top.astype(F32)).astype(BF16)
    return jnp.dot(jnp.concatenate([top, rest, top], axis=1), table, preferred_element_type=F32)


def grid_of(groups, ways):
    ny = max(ways // 2, 1)
    if groups % ny:
        ny = 1
    return ny, groups // ny


def last_group(i, ny, nz):
    z, y = i // ny, lax.rem(i, ny)
    far = jnp.where(2 * z < nz, nz - 1, 0)
    return far * ny + lax.rem(y + 1, ny)


def column_of(row, rows):
    lanes = row.shape[1]
    at = lax.broadcasted_iota(jnp.int32, (rows, lanes), 0) == lax.broadcasted_iota(jnp.int32, (rows, lanes), 1)
    return jnp.sum(jnp.where(at, jnp.broadcast_to(row, (rows, lanes)), 0.0), axis=1, keepdims=True)


def row_of(column, lanes):
    rows = column.shape[0]
    at = lax.broadcasted_iota(jnp.int32, (rows, lanes), 0) == lax.broadcasted_iota(jnp.int32, (rows, lanes), 1)
    return jnp.sum(jnp.where(at, jnp.broadcast_to(column, (rows, lanes)), 0.0), axis=0, keepdims=True)


def taps_spectrum(first, k_own, len_ref, xs, hs, f_table):
    share, taps = k_own.shape
    chunks = hs.shape[0]
    rows = share // chunks
    held = len_ref.shape[1]
    picked = lax.broadcasted_iota(jnp.int32, (share, held), 1) == first + lax.broadcasted_iota(jnp.int32, (share, held), 0)
    wide = jnp.broadcast_to(len_ref[...], (share, held)).astype(F32)
    lengths = jnp.sum(jnp.where(picked, wide, 0.0), axis=1, keepdims=True)
    kblocks = taps // BLOCK
    for c in range(kblocks):
        pos = (c * BLOCK + lax.broadcasted_iota(jnp.int32, (share, BLOCK), 1)).astype(F32)
        part = k_own[:, c * BLOCK:(c + 1) * BLOCK]
        part = jnp.where(pos < lengths, part, jnp.zeros_like(part))
        for h in range(chunks):
            xs[h, c * rows:(c + 1) * rows, :] = part[h * rows:(h + 1) * rows, :]
    for h in range(chunks):
        hs[h] = dot3(xs[h, :kblocks * rows, :], f_table[...])


def filter_rows(blocks, store, hs, xs, fs, ws, f_table, b_table):
    tblocks = len(blocks)
    rows = blocks[0].shape[0]
    kblocks = hs.shape[0] // rows
    for a in range(tblocks):
        xs[a * rows:(a + 1) * rows, :] = blocks[a]
    fs[...] = dot3(xs[:tblocks * rows, :], f_table[...])
    for b in range(tblocks):
        re = jnp.zeros((rows, BLOCK), F32)
        im = jnp.zeros((rows, BLOCK), F32)
        for c in range(min(b + 1, kblocks)):
            fr = fs[(b - c) * rows:(b - c + 1) * rows, :BLOCK]
            fi = fs[(b - c) * rows:(b - c + 1) * rows, BLOCK:]
            hr = hs[c * rows:(c + 1) * rows, :BLOCK]
            hi = hs[c * rows:(c + 1) * rows, BLOCK:]
            re = re + (fr * hr - fi * hi)
            im = im + (fr * hi + fi * hr)
        ws[b * rows:(b + 1) * rows, :BLOCK] = re
        ws[b * rows:(b + 1) * rows, BLOCK:] = im
    wide = dot3(ws[...], b_table[...])
    for b in range(tblocks):
        y = wide[b * rows:(b + 1) * rows, :BLOCK]
        if b:
            y = y + wide[(b - 1) * rows:b * rows, BLOCK:]
        store(b, y.astype(BF16))


def when(cond, body):
    if cond is None:
        body()
    else:
        pl.when(cond)(body)


def both(a, b):
    if a is None:
        return b
    return a if b is None else a & b


LEVELS = 32000.0


def main_kernel(
    ny, tile, a_hbm, p_hbm, k_hbm, len_hbm, s_hbm, g_hbm, ft_hbm, bt_hbm,
    acc_ref, big, slast_ref,
    a_ref, p_ref, len_ref, g_ref, f_table, b_table, in_sem,
    k_own, shapes, forces, fcore, coded, codes, scaled, scales, steps, fall, mod, xs, xf, fs, hs, ws, hot,
    k_sem, shape_sem, slast_sem, core_send, core_recv, code_send, code_recv, scale_send, scale_recv, own_sem,
    m_send, recv, s_up0, s_down0, s_y0, s_up, s_down, s_y, s_relief,
):
    groups, ways, chunks, rows, slab = big.shape
    share = chunks * rows
    halves = recv.shape[2]
    part = chunks // halves
    dofs = acc_ref.shape[0]
    per_group = ways * share
    nz = groups // ny
    split = shapes.shape[0] == groups
    i, j = lax.axis_index("mode"), lax.axis_index("tm")
    z, y = i // ny, lax.rem(i, ny)
    below, above = z > 0, z < nz - 1
    relief = ny == 2 and nz >= 4 and ways >= 4
    mate = j + 1 - 2 * lax.rem(j, 2)

    def peer(d):
        return lax.rem(j // 2 + d // 2, ways // 2) * 2 + lax.rem(lax.rem(j, 2) + d, 2)

    loads = [
        pltpu.make_async_copy(src, dst, in_sem.at[n])
        for n, (src, dst) in enumerate((
            (a_hbm, a_ref), (p_hbm, p_ref), (len_hbm, len_ref), (ft_hbm, f_table), (bt_hbm, b_table), (g_hbm, g_ref),
        ))
    ]
    first = j * share
    k_copy = pltpu.make_async_copy(k_hbm.at[pl.ds(pl.multiple_of(first, share), share)], k_own, k_sem)
    loads[0].start()
    loads[1].start()

    barrier = pltpu.get_barrier_semaphore()

    def greet(mode, tm):
        pl.semaphore_signal(barrier, inc=1, device_id={"mode": mode, "tm": tm}, device_id_type=MESH)

    for d in range(1, ways):
        greet(i, lax.rem(j + d, ways))
    for tm in (j, mate):
        for e in range(1, ny):
            greet(z * ny + lax.rem(y + e, ny), tm)
        if nz > 1:
            @pl.when(below)
            def _():
                greet(i - ny, tm)

            @pl.when(above)
            def _():
                greet(i + ny, tm)

    lanes = scaled.shape[2]
    pair = 2 * share
    loads[0].wait()
    loads[1].wait()

    def forces_of(chip):
        rows = p_ref[pl.ds(pl.multiple_of(chip * pair, pair), pair), :]
        return jnp.dot(rows, a_ref[...], preferred_element_type=F32)

    for c in range(1, ways // 2):
        chip = lax.rem(j // 2 + c, ways // 2)
        values = forces_of(chip)
        top = jnp.max(jnp.abs(values), axis=1, keepdims=True)
        scale = (top * 1.01 + 1e-30).astype(BF16).astype(F32)
        values = jnp.round(values * (LEVELS / scale)).astype(jnp.int32).astype(jnp.int16)
        for core in range(2):
            at = core * share
            line = row_of(scale[at:at + share, :], lanes)
            scaled[chip * 2 + core] = jnp.broadcast_to(line, scaled.shape[1:]).astype(BF16)
            for h in range(chunks):
                coded[chip * 2 + core, h] = values[at + h * rows:at + (h + 1) * rows, :]

    always = ways - 1 + 2 * (ny - 1)
    if nz == 1:
        pl.semaphore_wait(barrier, always)
    else:
        @pl.when(below & above)
        def _():
            pl.semaphore_wait(barrier, always + 4)

        @pl.when(jnp.logical_not(below & above))
        def _():
            pl.semaphore_wait(barrier, always + 2)

    started = []

    def remote(src, dst, send_sem, recv_sem, mode, tm):
        return pltpu.make_async_remote_copy(
            src, dst, send_sem, recv_sem, device_id={"mode": mode, "tm": tm}, device_id_type=MESH,
        )

    def code_copy(d, h):
        return remote(coded.at[peer(d), h], codes.at[d, h], code_send.at[d, h], code_recv.at[d, h], i, peer(d))

    def scale_copy(d):
        return remote(scaled.at[peer(d)], scales.at[d], scale_send.at[d], scale_recv.at[d], i, peer(d))

    core_copy = remote(forces.at[pl.ds(pl.multiple_of(lax.rem(mate, 2) * share, share), share)], fcore, core_send, core_recv, i, mate)
    for d in range(2, ways):
        scale_copy(d).start()
        started.append(functools.partial(scale_copy, d))
    for h in range(chunks):
        for d in range(2, ways):
            code_copy(d, h).start()
            started.append(functools.partial(code_copy, d, h))

    for load in loads[2:]:
        load.start()
    k_copy.start()
    forces[...] = forces_of(j // 2)
    core_copy.start()
    started.append(lambda: core_copy)

    def columns(g):
        return s_hbm.at[:, pl.ds(pl.multiple_of(g * per_group, per_group), per_group)]

    glast = last_group(i, ny, nz)
    shape_copies = []
    if split:
        for d in range(groups):
            g = lax.rem(i + d, groups)
            shape_copies.append(pltpu.make_async_copy(columns(g), shapes.at[g], shape_sem.at[d]))
        shape_copies.append(pltpu.make_async_copy(columns(glast), slast_ref, slast_sem))
    else:
        shape_copies.append(pltpu.make_async_copy(s_hbm, shapes.at[0], shape_sem.at[0]))
    for copy in shape_copies:
        copy.start()

    for load in loads[2:]:
        load.wait()
    k_copy.wait()
    taps_spectrum(first, k_own, len_ref, xs, hs, f_table)

    per = slab // BLOCK
    back = [d if d < 2 else (ways // 2 - d // 2) * 2 + d % 2 for d in range(ways)]
    for d in range(2, ways):
        scale_copy(d).wait_recv()
    for d in range(2, ways):
        column = column_of(scales[back[d], 0:1, :].astype(F32), share) * (1 / LEVELS)
        for h in range(chunks):
            steps[d, h] = jnp.broadcast_to(column[h * rows:(h + 1) * rows, :], steps.shape[2:])
    core_copy.wait_recv()

    def hops(h):
        dst, sem = big.at[i, j, h], recv.at[i, j, h // part]
        made = []
        for d in range(2, ways):
            made.append((None, remote(mod.at[h, peer(d)], dst, m_send.at[d, h], sem, i, peer(d))))
        for n, tm in enumerate((j, mate)):
            src = mod.at[h, tm]
            for e in range(1, ny):
                made.append((None, remote(src, dst, s_y0.at[e - 1, n, h], sem, z * ny + lax.rem(y + e, ny), tm)))
            if nz > 1:
                made.append((above, remote(src, dst, s_up0.at[n, h], sem, i + ny, tm)))
                made.append((below, remote(src, dst, s_down0.at[n, h], sem, i - ny, tm)))
        made.append((None, remote(mod.at[h, mate], dst, m_send.at[1, h], sem, i, mate)))
        return made

    def chunk(h, carry):
        for d in range(2, ways):
            code_copy(d, h).wait_recv()
        at = pl.ds(pl.multiple_of(h * rows, rows), rows)
        fall[j] = forces[pl.ds(pl.multiple_of(lax.rem(j, 2) * share + h * rows, rows), rows), :]
        fall[mate] = fcore[at, :]
        for d in range(2, ways):
            fall[peer(d)] = codes[back[d], h].astype(jnp.int32).astype(F32) * steps[d, h, :, 0:1]
        blocks = [fall[b // per, :, (b % per) * BLOCK:(b % per + 1) * BLOCK] for b in range(ways * per)]

        def store(b, value):
            mod[h, b // per, :, (b % per) * BLOCK:(b % per + 1) * BLOCK] = value

        filter_rows(blocks, store, hs.at[h], xf, fs, ws, f_table, b_table)
        for cond, copy in hops(h):
            when(cond, copy.start)
        big[i, j, h] = mod[h, j]
        return carry

    lax.fori_loop(0, chunks, chunk, 0)

    pending = []

    def half(g, q, k):
        return big.at[g, q, pl.ds(k * part, part)]

    def send(cond, g, q, k, sem, mode, tm):
        def make():
            return remote(half(g, q, k), half(g, q, k), sem.at[k], recv.at[g, q, k], mode, tm)
        when(cond, lambda: make().start())
        pending.append((cond, make))

    def sent(n):
        for cond, make in pending[:n]:
            when(cond, lambda: make().wait_send())
        del pending[:n]

    def arrived(cond, g, q, k):
        when(cond, lambda: remote(half(g, q, k), half(g, q, k), own_sem, recv.at[g, q, k], i, j).wait_recv())

    lane = g_ref.shape[1]
    work = collections.deque()

    def ground(r):
        for part in range(tile // lane):
            at = r * (tile // lane) + part
            column = column_of(g_ref[at:at + 1, :].astype(F32), lane)
            support = lax.broadcasted_iota(jnp.int32, (lane, a_ref.shape[0]), 1).astype(F32)
            hot[part * lane:(part + 1) * lane, :] = (support == column).astype(F32).astype(BF16)
        acc_ref[r * tile:(r + 1) * tile, :] = jnp.dot(hot[...], a_ref[...], preferred_element_type=F32)

    for r in range(dofs // tile):
        work.append((None, functools.partial(ground, r)))

    def product(cond, g):
        if not split:
            return

        def unit(r):
            at = pl.ds(r * tile, tile)
            block = big[g].reshape(per_group, slab)
            acc_ref[at, :] += jnp.dot(shapes[g, at, :], block, preferred_element_type=F32)
        for r in range(dofs // tile):
            work.append((cond, functools.partial(unit, r)))

    def drain(n):
        for _ in range(min(n, len(work))):
            cond, unit = work.popleft()
            when(cond, unit)

    def across(cond, g, q, k, slot, d):
        for e in range(1, ny):
            send(cond, g, q, k, s_y.at[slot, e - 1, d], z * ny + lax.rem(y + e, ny), j)

    def up(cond, g, q, k, slot, d):
        if nz > 1:
            send(both(cond, above), g, q, k, s_up.at[slot, d], i + ny, j)

    def down(cond, g, q, k, slot, d):
        if nz > 1:
            send(both(cond, below), g, q, k, s_down.at[slot, d], i - ny, j)

    def own_event(d, k):
        q = peer(d)
        arrived(None, i, q, k)
        if d >= 2:
            across(None, i, q, k, 0, d)
            down(None, i, q, k, 0, d)
            up(None, i, q, k, 0, d)

    def column_event(s, d, k):
        q = peer(d)
        lower, upper = i - s * ny, i + s * ny
        has_low, has_high = z - s >= 0, z + s <= nz - 1
        far = relief and s == nz - 1 and 2 * (d * halves + k) >= ways * halves + 2 * (ways * halves // 8)
        near = relief and s == 1
        arrived(has_high, upper, q, k)
        if not far:
            across(both(has_high, z != nz - 2 if near else None), upper, q, k, nz - 1 + s, d)
        down(has_high, upper, q, k, s, d)
        arrived(has_low, lower, q, k)
        if not far:
            across(both(has_low, z != 1 if near else None), lower, q, k, s, d)
        up(has_low, lower, q, k, s, d)

    def other_event(s, d, k):
        q = peer(d)
        for e in range(1, ny):
            line = lax.rem(y + e, ny)
            if s == 0:
                g = z * ny + line
                arrived(None, g, q, k)
                if relief:
                    send(z == 0, g, q, k, s_relief.at[0, d], i + ny, j)
                    send(z == nz - 1, g, q, k, s_relief.at[0, d], i - ny, j)
                continue
            lower, upper = (z - s) * ny + line, (z + s) * ny + line
            arrived(z - s >= 0, lower, q, k)
            arrived(z + s <= nz - 1, upper, q, k)
            if relief and s == nz - 2 and 2 * (d * halves + k) >= ways * halves + 2 * (ways * halves // 8):
                send(z == nz - 2, lower, q, k, s_relief.at[1, d], i + ny, j)
                send(z == 1, upper, q, k, s_relief.at[1, d], i - ny, j)

    def other_products(s):
        for e in range(1, ny):
            line = lax.rem(y + e, ny)
            if s == 0:
                g = z * ny + line
                product(g != glast, g)
                continue
            for level, there in ((z - s, z - s >= 0), (z + s, z + s <= nz - 1)):
                g = level * ny + line
                product(there & (g != glast), g)

    for copy in shape_copies:
        copy.wait()
    near_ones, far_ones = range(min(2, ways)), range(2, ways)
    for k in range(halves):
        for d in near_ones:
            if nz > 1:
                column_event(1, d, k)
            for f in far_ones:
                if f % 2 == d:
                    own_event(f, k)
        own_event(1, k)
        for d in near_ones:
            other_event(0, d, k)
        drain(1)
    product(None, i)
    for k in range(halves):
        for d in far_ones:
            if nz > 1:
                column_event(1, d, k)
            other_event(0, d, k)
            drain(1)
    before = len(pending)
    for s in range(2, nz):
        product(z - s + 1 >= 0, i - (s - 1) * ny)
        product(z + s - 1 <= nz - 1, i + (s - 1) * ny)
        other_products(s - 2)
        if s == 2:
            for make in started:
                make().wait_send()

            def hopped(h, carry):
                for cond, copy in hops(h):
                    when(cond, copy.wait_send)
                return carry

            lax.fori_loop(0, chunks, hopped, 0)
        else:
            sent(before)
            before = len(pending)
        for some in (near_ones, far_ones):
            for k in range(halves):
                for d in some:
                    column_event(s, d, k)
                    other_event(s - 1, d, k)
                    drain(1)
    if nz > 1:
        s = nz - 1
        product(z - s >= 0, i - s * ny)
        product(z + s <= nz - 1, i + s * ny)
    other_products(max(nz - 2, 0))
    drain(len(work))
    if nz <= 2:
        for make in started:
            make().wait_send()
        for h in range(chunks):
            for cond, copy in hops(h):
                when(cond, copy.wait_send)
    sent(before)
    if nz > 1:
        for d in range(ways):
            for k in range(halves):
                other_event(nz - 1, d, k)
        other_products(nz - 1)
    drain(len(work))
    if not split:
        def whole(r, carry):
            at = pl.ds(pl.multiple_of(r * tile, tile), tile)
            block = big[...].reshape(groups * per_group, slab)
            acc_ref[at, :] += jnp.dot(shapes[0, at, :], block, preferred_element_type=F32)
            return carry
        lax.fori_loop(0, dofs // tile, whole, 0)
    sent(len(pending))


def tail_kernel(ny, tile, acc_ref, big, s_ref, o_hbm, out, sem):
    groups, ways, chunks, rows, slab = big.shape
    glast = last_group(lax.axis_index("mode"), ny, groups // ny)
    dofs = acc_ref.shape[0]
    copies = []
    for n in range(dofs // tile):
        at = pl.ds(n * tile, tile)
        total = acc_ref[at, :]
        if s_ref.shape[0] == dofs:
            block = big[glast].reshape(ways * chunks * rows, slab)
            total += jnp.dot(s_ref[at, :], block, preferred_element_type=F32)
        out[at, :] = total.astype(BF16)
        copies.append(pltpu.make_async_copy(out.at[at], o_hbm.at[at], sem.at[n]))
        copies[-1].start()
    for copy in copies:
        copy.wait()


def per_device(support_accel, participation, kernels, lengths, mode_shapes, groups):
    ways, ngroups = lax.axis_size("tm"), lax.axis_size("mode")
    ny, nz = grid_of(ngroups, ways)
    held, taps = kernels.shape
    share = held // ways
    rows = 16 if share % 16 == 0 else share
    chunks = share // rows
    halves = 2 if chunks % 2 == 0 else 1
    supports, slab = support_accel.shape
    dofs, modes = mode_shapes.shape
    tile = min(1024, dofs)
    last_tile = min(512, dofs)
    split = held % 128 == 0 and ny > 1 and dofs > tile
    times = ways * slab
    lanes = -(-share // 128) * 128
    tables = transform_tables()
    hbm = pl.BlockSpec(memory_space=pltpu.HBM)
    vmem = pl.BlockSpec(memory_space=pltpu.VMEM)
    dma = pltpu.SemaphoreType.DMA
    acc, every, shapes = pl.pallas_call(
        functools.partial(main_kernel, ny, tile),
        out_shape=(
            pltpu.VMEM((dofs, slab), F32),
            pltpu.VMEM((ngroups, ways, chunks, rows, slab), BF16),
            pltpu.VMEM((dofs, held) if split else (16, 128), BF16),
        ),
        in_specs=[hbm] * 8,
        out_specs=(vmem, vmem, vmem),
        scratch_shapes=[
            pltpu.VMEM((supports, slab), BF16),
            pltpu.VMEM((held, supports), BF16),
            pltpu.VMEM((1, held), jnp.int32),
            pltpu.VMEM((dofs // 128, 128), jnp.int32),
            *(pltpu.VMEM(table.shape, BF16) for table in tables),
            dma((6,)),
            pltpu.VMEM((share, taps), F32),
            pltpu.VMEM((ngroups, dofs, held) if split else (1, dofs, modes), BF16),
            pltpu.VMEM((2 * share, slab), F32),
            pltpu.VMEM((share, slab), F32),
            pltpu.VMEM((ways, chunks, rows, slab), jnp.int16),
            pltpu.VMEM((ways, chunks, rows, slab), jnp.int16),
            pltpu.VMEM((ways, 16, lanes), BF16),
            pltpu.VMEM((ways, 16, lanes), BF16),
            pltpu.VMEM((ways, chunks, rows, 128), F32),
            pltpu.VMEM((ways, rows, slab), F32),
            pltpu.VMEM((chunks, ways, rows, slab), BF16),
            pltpu.VMEM((chunks, taps // BLOCK * rows, BLOCK), F32),
            pltpu.VMEM((times // BLOCK * rows, BLOCK), F32),
            pltpu.VMEM((times // BLOCK * rows, 2 * BLOCK), F32),
            pltpu.VMEM((chunks, taps // BLOCK * rows, 2 * BLOCK), F32),
            pltpu.VMEM((times // BLOCK * rows, 2 * BLOCK), F32),
            pltpu.VMEM((tile, supports), BF16),
            dma, dma((ngroups,)), dma, dma, dma, dma((ways, chunks)), dma((ways, chunks)), dma((ways,)), dma((ways,)), dma,
            dma((ways, chunks)), dma((ngroups, ways, halves)),
            dma((2, chunks)), dma((2, chunks)), dma((max(ny - 1, 1), 2, chunks)),
            dma((nz, ways, halves)), dma((nz, ways, halves)), dma((2 * nz - 1, max(ny - 1, 1), ways, halves)),
            dma((2, ways, halves)),
        ],
        compiler_params=pltpu.CompilerParams(
            collective_id=0, has_side_effects=True, vmem_limit_bytes=40 << 20
        ),
    )(*(pltpu.with_memory_space_constraint(array, pltpu.HBM) for array in (
        support_accel, participation, kernels, lengths.reshape(1, held), mode_shapes,
        groups.reshape(dofs // 128, 128), *map(jnp.asarray, tables),
    )))
    return pl.pallas_call(
        functools.partial(tail_kernel, ny, last_tile),
        out_shape=jax.ShapeDtypeStruct((dofs, slab), BF16),
        in_specs=[vmem, vmem, vmem],
        out_specs=hbm,
        scratch_shapes=[pltpu.VMEM((dofs, slab), BF16), dma((dofs // last_tile,))],
        compiler_params=pltpu.CompilerParams(vmem_limit_bytes=24 << 20),
    )(acc, every, shapes)


def solution(mesh):
    placed = (
        P(None, "tm"),
        P("mode", None),
        P("mode", None),
        P("mode"),
        P("mode", None),
        P("mode"),
    )
    return jax.shard_map(
        per_device, mesh=mesh, in_specs=placed, out_specs=P("mode", "tm"), check_vma=False
    )
```
